128 devices in a mesh: dp: 16 (over z, x_lo, core), space: 8 (over x_hi, y).
Axes of the slice: x: 4 (x_hi: 2, x_lo: 2; x = x_hi * 2 + x_lo), y: 4, z: 4, core: 2. Of those that a mesh axis runs over, the one named last changes fastest.
Arguments:
- features: bfloat16 [16, 128, 64, 1024], P('dp', 'space'), may hold values from -6 to 6
- target: bfloat16 [16, 128, 64, 1024], P('dp', 'space'), may hold values from -6 to 6
- anchors: int32 [16, 2], P('dp'), may hold values from 0 to 64512
- w_first: bfloat16 [3, 3, 64, 64], replicated, may hold values from -0.25 to 0.25
- b_first: float32 [64], replicated, may hold values from -3 to 3
- w_second: bfloat16 [3, 3, 64, 64], replicated, may hold values from -0.25 to 0.25
- b_second: float32 [64], replicated, may hold values from -3 to 3
Outputs:
- back_input: bfloat16 [16, 128, 64, 1024], P('dp', 'space')
- grad_w1: float32 [3, 3, 64, 64], replicated
- grad_b1: float32 [64], replicated
- grad_w2: float32 [3, 3, 64, 64], replicated
- grad_b2: float32 [64], replicated
The draws below stay inside these ranges and needn't reach their ends.
All inputs are finite; a program needn't handle non-finite values.
Results may differ from the reference program's by a relative error of at most 0.0075.
Values may be sent and summed in bfloat16 or wider, within the bound.
No kernel may reach another device: no remote copies, remote signals or barrier semaphores. Data moves between devices by JAX's collectives and lax.ppermute only.
A program may use at most 128 MiB of HBM per device.

```python
import math
import jax
import jax.numpy as jnp
from jax import lax

CH = 64
COLS = 1024
GRID = 65536
H = 128
CROPS = 16


def touch_ends(entries, own_key, low, largest):
    extent = entries.shape
    spot = [jax.random.randint(jax.random.fold_in(own_key, axis), (), 0, extent[axis]) for axis in range(len(extent))]
    entries = entries.at[tuple(spot)].set(low)
    longest = extent.index(max(extent))
    spot[longest] = (spot[longest] + 1) % extent[longest]
    return entries.at[tuple(spot)].set(largest)


def steps_of(own_key, dims, shards, smallest, high):
    gain, own = 1.0, jax.random.fold_in(own_key, 6)
    for axis_at, parts in shards:
        draws = jnp.exp(jax.random.uniform(jax.random.fold_in(own, axis_at), (parts,), jnp.float32, smallest / len(shards), high / len(shards)))
        gain = gain * jnp.repeat(draws, dims[axis_at] // parts).reshape([-1 if axis == axis_at else 1 for axis in range(len(dims))])
    return gain


def normal_values(key, extent, deviation, limit, shards=(), kind=jnp.bfloat16):
    array = jax.random.normal(key, extent, jnp.float32) * deviation
    if len(shards) > 0:
        array = steps_of(key, extent, shards, -0.22, 0.18) * array
    return jnp.clip(array, min=-limit, max=limit).astype(kind)


def setup_inputs(seed: int = 0) -> dict:
    splits = jax.random.split(jax.random.key(seed), 8)
    features = normal_values(splits[0], (CROPS, H, CH, COLS), 1.0, 6.0, ((0, 16), (1, 8)))
    target = normal_values(splits[1], (CROPS, H, CH, COLS), 1.0, 6.0, ((0, 16), (1, 8)))
    anchors = touch_ends(jax.random.randint(splits[2], (CROPS, 2), 0, GRID - max(H, COLS) + 1), jax.random.fold_in(splits[2], 1), 0, GRID - max(H, COLS)).astype(jnp.int32)
    w_first = normal_values(splits[3], (3, 3, CH, CH), (9 * CH) ** -0.5, 0.25)
    b_first = normal_values(splits[4], (CH,), 0.5, 3.0, (), jnp.float32)
    w_second = normal_values(splits[5], (3, 3, CH, CH), (9 * CH) ** -0.5, 0.25)
    b_second = normal_values(splits[6], (CH,), 0.5, 3.0, (), jnp.float32)
    return dict(features=features, target=target, anchors=anchors, w_first=w_first, b_first=b_first, w_second=w_second, b_second=b_second)


def shift_cols(tensor, offset):
    if offset == 0:
        return tensor
    filler = jnp.zeros(tensor.shape[:-1] + (1,), tensor.dtype)
    if offset > 0:
        return jnp.concatenate([tensor[..., 1:], filler], axis=-1)
    return jnp.concatenate([filler, tensor[..., :-1]], axis=-1)

def unfold(padded):
    inner = padded.shape[1] - 2
    pieces = [shift_cols(padded[:, row_off:row_off + inner], col_off - 1) for row_off in range(3) for col_off in range(3)]
    return jnp.concatenate(pieces, axis=2)

def unfold_back(padded):
    inner = padded.shape[1] - 2
    pieces = [shift_cols(padded[:, 2 - row_off:2 - row_off + inner], 1 - col_off) for row_off in range(3) for col_off in range(3)]
    return jnp.concatenate(pieces, axis=2)

def forward_matrix(kernel):
    return jnp.transpose(kernel, (2, 0, 1, 3)).reshape(kernel.shape[2], -1)

def backward_matrix(kernel):
    return jnp.transpose(kernel, (3, 0, 1, 2)).reshape(kernel.shape[3], -1)

def fold_kernel(matrix):
    channels = matrix.shape[0]
    return jnp.transpose(matrix.reshape(channels, 3, 3, -1), (1, 2, 0, 3))

def coords(anchor_rows, row_ids, columns, channels):
    chan_ids = jnp.arange(channels, dtype=jnp.int32)
    periods = 4 * jnp.left_shift(jnp.ones_like(chan_ids), chan_ids % 8)
    scaled = 2.0 * math.pi / periods.astype(jnp.float32)
    row_pos = anchor_rows[:, 0][:, None, None] + row_ids.astype(jnp.int32)[None, :, None]
    row_wave = jnp.sin((row_pos % periods[None, None, :]).astype(jnp.float32) * scaled[None, None, :])
    col_ids = jnp.arange(columns, dtype=jnp.int32)
    col_pos = anchor_rows[:, 1][:, None, None] + col_ids[None, None, :]
    col_wave = jnp.sin((col_pos % periods[None, :, None]).astype(jnp.float32) * scaled[None, :, None])
    use_rows = (chan_ids < channels // 2)[None, None, :, None]
    return jnp.where(use_rows, row_wave[..., None], col_wave[:, None])

def gelu_grad(pre_act, upstream):
    return jax.vjp(lambda inputs: jax.nn.gelu(inputs, approximate=True), pre_act)[1](upstream)[0]

def mixing(form, left, right):
    return jnp.einsum(form, left.astype(jnp.float32), right.astype(jnp.float32), precision=lax.Precision.HIGHEST)

def pad_rows(field):
    return jnp.pad(field, ((0, 0), (1, 1), (0, 0), (0, 0)))

def reference(features, target, anchors, w_first, b_first, w_second, b_second):

    def one_crop(items):
        crop, goal, anchor = items
        geo = coords(anchor[None], jnp.arange(H, dtype=jnp.int32), COLS, CH)
        first = (crop[None].astype(jnp.float32) + geo).astype(jnp.bfloat16)
        first_pad = pad_rows(first)
        pre_act = mixing('dk,brkw->brdw', forward_matrix(w_first), unfold(first_pad)) + b_first[None, None, :, None]
        hidden = jax.nn.gelu(pre_act, approximate=True).astype(jnp.bfloat16)
        hidden_pad = pad_rows(hidden)
        output = mixing('dk,brkw->brdw', forward_matrix(w_second), unfold(hidden_pad)) + b_second[None, None, :, None]
        misfit = (output - goal[None].astype(jnp.float32)).astype(jnp.bfloat16)
        grad_w2 = fold_kernel(mixing('brdw,brkw->dk', misfit, unfold(hidden_pad)))
        grad_b2 = lax.optimization_barrier(jnp.sum(misfit.astype(jnp.float32), axis=(0, 1, 3)))
        back_hidden = mixing('ck,brkw->brcw', backward_matrix(w_second), unfold_back(pad_rows(misfit)))
        slope = gelu_grad(pre_act, back_hidden).astype(jnp.bfloat16)
        grad_w1 = fold_kernel(mixing('brdw,brkw->dk', slope, unfold(first_pad)))
        grad_b1 = lax.optimization_barrier(jnp.sum(slope.astype(jnp.float32), axis=(0, 1, 3)))
        back_input = mixing('ck,brkw->brcw', backward_matrix(w_first), unfold_back(pad_rows(slope))).astype(jnp.bfloat16)
        return (back_input[0], grad_w1, grad_b1, grad_w2, grad_b2)
    results = lax.map(one_crop, (features, target, anchors))
    factor = 1.0 / math.sqrt(CROPS * H * COLS)
    return (results[0], lax.optimization_barrier(jnp.sum(results[1], axis=0)) * factor, lax.optimization_barrier(jnp.sum(results[2], axis=0)) * factor, lax.optimization_barrier(jnp.sum(results[3], axis=0)) * factor, lax.optimization_barrier(jnp.sum(results[4], axis=0)) * factor)
```

```python
import functools
import math

import jax
import jax.numpy as jnp
from jax import lax
from jax.experimental import pallas as pl
from jax.experimental.pallas import tpu as pltpu
from jax.sharding import PartitionSpec as P

BF = jnp.bfloat16
F32 = jnp.float32
AXES = ("dp", "space")
FEAT_HALO = 4
GOAL_HALO = 2
GELU_SCALE = math.sqrt(2.0 / math.pi)
GELU_CUBE = 0.044715


def to_right(value):
    lane = lax.broadcasted_iota(jnp.int32, value.shape, 1)
    return jnp.where(lane == 0, jnp.zeros_like(value), pltpu.roll(value, 1, 1))


def to_left(value):
    last = value.shape[1] - 1
    lane = lax.broadcasted_iota(jnp.int32, value.shape, 1)
    return jnp.where(lane == last, jnp.zeros_like(value), pltpu.roll(value, last, 1))


def keep(flag, value):
    return jnp.where(flag > 0, value, jnp.zeros_like(value))


def masked(value, low, high):
    if low is None and high is None:
        return value
    half = value.shape[0] // 2
    first, second = value[:half], value[half:]
    if low is not None:
        first = keep(low, first)
    if high is not None:
        second = keep(high, second)
    return jnp.concatenate([first, second], axis=0)


def lane_sum(value):
    half = value.shape[0] // 2
    both = value[:half] + value[half:]
    total = both[:, :128]
    for start in range(128, both.shape[1], 128):
        total = total + both[:, start : start + 128]
    return total


def step_kernel(
    rows,
    ch,
    factor,
    flags_ref,
    feat_ref,
    goal_ref,
    top_ref,
    bot_ref,
    row_wave_ref,
    col_wave_ref,
    fwd1_ref,
    fwd2_ref,
    bwd1_ref,
    bwd2_ref,
    bias1_ref,
    bias2_ref,
    back_ref,
    grads_ref,
    first,
    hidden,
    deriv,
    misfit,
    slope,
    acc1,
    acc2,
    sum1,
    sum2,
):
    pair = 2 * ch
    quad = 4 * ch
    cols = feat_ref.shape[-1]
    above, below = flags_ref[0], flags_ref[1]

    def put_first(index, value, flag):
        wave = jnp.concatenate(
            [
                jnp.tile(row_wave_ref[index], (1, cols // 128)),
                col_wave_ref[...],
            ],
            axis=0,
        )
        result = value.astype(F32) + wave
        if flag is not None:
            result = keep(flag, result)
        first[pl.ds(pl.multiple_of(index * ch, ch), ch)] = result.astype(BF)

    for row in range(FEAT_HALO):
        put_first(row, top_ref[row], above)
        put_first(rows + FEAT_HALO + row, bot_ref[row], below)

    def put_inner(row, carry):
        put_first(row + FEAT_HALO, feat_ref[row], None)
        return carry

    lax.fori_loop(0, rows, put_inner, 0, unroll=2)

    bias1 = jnp.broadcast_to(bias1_ref[...], (pair, cols))
    bias2 = jnp.broadcast_to(bias2_ref[...], (pair, cols))

    def spread(kernel_ref, source, at):
        parts = jnp.dot(
            kernel_ref[...],
            source[pl.ds(pl.multiple_of(at * ch, ch), quad)],
            preferred_element_type=F32,
        )
        return parts[pair : 2 * pair] + to_right(parts[:pair]) + to_left(parts[2 * pair :])

    def forward_one(p, low, high, wants_deriv):
        pre = spread(fwd1_ref, first, 2 * p) + bias1_ref[...]
        square = pre * pre
        bent = jnp.tanh(pre * (GELU_SCALE + (GELU_SCALE * GELU_CUBE) * square))
        cdf = 0.5 + 0.5 * bent
        hid = masked(pre * cdf, low, high)
        hidden[pl.ds(pl.multiple_of(p * pair, pair), pair)] = hid.astype(BF)
        if wants_deriv:
            inner = GELU_SCALE + (3.0 * GELU_SCALE * GELU_CUBE) * square
            grad = cdf + (0.5 * pre) * ((1.0 - bent * bent) * inner)
            deriv[pl.ds(pl.multiple_of((p - 1) * pair, pair), pair)] = grad

    def put_three(target, at, value):
        spot = pl.ds(pl.multiple_of(at * ch, ch), pair)
        target[0, spot] = to_left(value)
        target[1, spot] = value
        target[2, spot] = to_right(value)

    def forward_two(p, goal, flag):
        out = spread(fwd2_ref, hidden, 2 * p) + bias2_ref[...]
        error = out - goal.astype(F32)
        if flag is not None:
            error = keep(flag, error)
        error = error.astype(BF)
        put_three(misfit, 2 * p, error)
        if flag is None:
            sum2[...] += lane_sum(error.astype(F32))

    def back(kernel_ref, source, at):
        spot = pl.ds(pl.multiple_of(at * ch, ch), quad)
        stack = jnp.concatenate([source[0, spot], source[1, spot], source[2, spot]], axis=0)
        return jnp.dot(kernel_ref[...], stack, preferred_element_type=F32)

    def backward_two(p, low, high):
        up = back(bwd2_ref, misfit, 2 * p)
        value = up * deriv[pl.ds(pl.multiple_of(p * pair, pair), pair)]
        value = masked(value, low, high).astype(BF)
        put_three(slope, 2 * p, value)
        wide = value.astype(F32)
        half = wide.shape[0] // 2
        if low is not None:
            wide = jnp.concatenate([jnp.zeros_like(wide[:half]), wide[half:]], axis=0)
        if high is not None:
            wide = jnp.concatenate([wide[:half], jnp.zeros_like(wide[half:])], axis=0)
        sum1[...] += lane_sum(wide)

    def backward_one(p):
        value = back(bwd1_ref, slope, 2 * p).astype(BF)
        back_ref[2 * p] = value[:ch]
        back_ref[2 * p + 1] = value[ch:]

    def weight_grad(acc, errors, error_at, source, source_at):
        spot = pl.ds(pl.multiple_of(error_at * ch, ch), pair)
        stack = jnp.concatenate([errors[0, spot], errors[1, spot], errors[2, spot]], axis=0)
        block = source[pl.ds(pl.multiple_of(source_at * ch, ch), quad)]
        acc[...] += lax.dot_general(
            stack, block, (((1,), (1,)), ((), ())), preferred_element_type=F32
        )

    sum1[...] = jnp.zeros_like(sum1)
    sum2[...] = jnp.zeros_like(sum2)
    acc1[...] = jnp.zeros_like(acc1)
    acc2[...] = jnp.zeros_like(acc2)

    def loop(start, stop, body, unroll):
        def run(p, carry):
            body(p)
            return carry

        lax.fori_loop(start, stop, run, 0, unroll=unroll)

    pairs = rows // 2
    forward_one(0, above, above, False)
    forward_one(1, above, None, True)
    loop(2, pairs + 1, lambda p: forward_one(p, None, None, True), 7)
    forward_one(pairs + 1, None, below, True)
    forward_one(pairs + 2, below, below, False)

    def goal_rows(at):
        return jnp.concatenate([goal_ref[at], goal_ref[at + 1]], axis=0)

    forward_two(0, jnp.concatenate([top_ref[4], top_ref[5]], axis=0), above)
    forward_two(pairs + 1, jnp.concatenate([bot_ref[4], bot_ref[5]], axis=0), below)
    loop(1, pairs + 1, lambda p: forward_two(p, goal_rows(2 * p - 2), None), 4)

    loop(0, pairs, lambda p: weight_grad(acc2, misfit, 2 * p + 2, hidden, 2 * p + 2), 4)

    backward_two(0, above, None)
    backward_two(pairs, None, below)
    loop(1, pairs, lambda p: backward_two(p, None, None), 7)

    loop(0, pairs, lambda p: weight_grad(acc1, slope, 2 * p + 1, first, 2 * p + 3), 4)
    loop(0, pairs, backward_one, 4)

    def emit(base, acc, total):
        summed = jnp.sum(total[...], axis=1, keepdims=True)
        side = jnp.broadcast_to(summed, (ch, ch))
        for j in range(3):
            low = acc[2 * j * ch : (2 * j + 1) * ch]
            high = acc[(2 * j + 1) * ch : (2 * j + 2) * ch]
            block = jnp.concatenate([low[:, : 3 * ch] + high[:, ch:], side], axis=1) * factor
            for t in range(ch // 8):
                for half in range(2):
                    grads_ref[base + (j * (ch // 8) + t) * 2 + half] = block[
                        8 * t : 8 * t + 8, 128 * half : 128 * half + 128
                    ]

    emit(0, acc1, sum1)
    emit(6 * (ch // 8), acc2, sum2)
    for spare in range(12 * (ch // 8), grads_ref.shape[0]):
        grads_ref[spare] = jnp.zeros((8, 128), F32)


def split_kernel(ch, full_ref, w1_ref, b1_ref, w2_ref, b2_ref):
    for base, w_ref, b_ref in ((0, w1_ref, b1_ref), (6 * (ch // 8), w2_ref, b2_ref)):
        for j in range(3):
            left, right = [
                jnp.concatenate(
                    [full_ref[base + (j * (ch // 8) + t) * 2 + half] for t in range(ch // 8)],
                    axis=0,
                )
                for half in range(2)
            ]
            w_ref[0, j] = left[:, :ch]
            w_ref[1, j] = left[:, ch:]
            w_ref[2, j] = right[:, :ch]
            if j == 0:
                b_ref[...] = jnp.transpose(right)[ch : ch + 8]


def pair_matrix(kernel, order):
    ch = kernel.shape[-1]
    flat = jnp.transpose(kernel, order).reshape(3, ch, 3 * ch)
    low = jnp.pad(flat, ((0, 0), (0, 0), (0, ch)))
    high = jnp.pad(flat, ((0, 0), (0, 0), (ch, 0)))
    return jnp.stack([low, high], axis=1).reshape(3, 2 * ch, 4 * ch)


def forward_matrix(kernel):
    matrix = pair_matrix(kernel, (1, 2, 0, 3))
    return matrix.reshape(-1, matrix.shape[-1])


def backward_matrix(kernel):
    matrix = pair_matrix(kernel[::-1], (1, 3, 0, 2))
    return jnp.transpose(matrix, (1, 0, 2)).reshape(matrix.shape[1], -1)


def waves(anchors, row_ids, columns, channels):
    chan_ids = jnp.arange(channels, dtype=jnp.int32)
    periods = 4 * jnp.left_shift(jnp.ones_like(chan_ids), chan_ids % 8)
    scaled = 2.0 * math.pi / periods.astype(F32)
    half = channels // 2
    row_pos = anchors[0, 0] + row_ids[:, None]
    row_wave = jnp.sin(
        jnp.remainder(row_pos, periods[None, :half]).astype(F32) * scaled[None, :half]
    )
    col_pos = anchors[0, 1] + jnp.arange(columns, dtype=jnp.int32)[None, :]
    col_wave = jnp.sin(
        jnp.remainder(col_pos, periods[half:, None]).astype(F32) * scaled[half:, None]
    )
    return jnp.broadcast_to(row_wave[:, :, None], row_wave.shape + (128,)), col_wave


def shards(features, target, anchors, w_first, b_first, w_second, b_second):
    _, rows, ch, cols = features.shape
    size = lax.axis_size("space")
    devices = size * lax.axis_size("dp")
    me = lax.axis_index("space")
    factor = 1.0 / math.sqrt(features.shape[0] * devices * rows * cols)
    feats, goals = features[0], target[0]
    down = [(i, i + 1) for i in range(size - 1)]
    up = [(i + 1, i) for i in range(size - 1)]
    top = lax.ppermute(
        jnp.concatenate([feats[rows - FEAT_HALO :], goals[rows - GOAL_HALO :]]), "space", down
    )
    bottom = lax.ppermute(jnp.concatenate([feats[:FEAT_HALO], goals[:GOAL_HALO]]), "space", up)
    ids = me * rows - FEAT_HALO + jnp.arange(rows + 2 * FEAT_HALO, dtype=jnp.int32)
    row_wave, col_wave = waves(anchors, ids, cols, ch)
    flags = jnp.stack([me > 0, me < size - 1]).astype(jnp.int32)
    vmem = pl.BlockSpec(memory_space=pltpu.VMEM)
    smem = pl.BlockSpec(memory_space=pltpu.SMEM)
    pair, quad = 2 * ch, 4 * ch
    back, grads = pl.pallas_call(
        functools.partial(step_kernel, rows, ch, factor),
        out_shape=(
            jax.ShapeDtypeStruct((rows, ch, cols), BF),
            jax.ShapeDtypeStruct((devices, 8, 128), F32),
        ),
        in_specs=[smem] + [vmem] * 12,
        out_specs=(vmem, vmem),
        scratch_shapes=[
            pltpu.VMEM(((rows + 8) * ch, cols), BF),
            pltpu.VMEM(((rows + 6) * ch, cols), BF),
            pltpu.VMEM(((rows + 2) * ch, cols), F32),
            pltpu.VMEM((3, (rows + 4) * ch, cols), BF),
            pltpu.VMEM((3, (rows + 2) * ch, cols), BF),
            pltpu.VMEM((3 * pair, quad), F32),
            pltpu.VMEM((3 * pair, quad), F32),
            pltpu.VMEM((ch, 128), F32),
            pltpu.VMEM((ch, 128), F32),
        ],
        compiler_params=pltpu.CompilerParams(vmem_limit_bytes=58 << 20),
        name="step",
    )(
        flags,
        feats,
        goals,
        top,
        bottom,
        row_wave,
        col_wave,
        forward_matrix(w_first),
        forward_matrix(w_second),
        backward_matrix(w_first),
        backward_matrix(w_second),
        jnp.tile(b_first, 2)[:, None],
        jnp.tile(b_second, 2)[:, None],
    )
    parts = lax.all_to_all(grads, AXES, 0, 0, tiled=True)
    mine = jnp.sum(parts, axis=0)
    full = lax.all_to_all(
        jnp.broadcast_to(mine[None], (devices, 8, 128)), AXES, 0, 0, tiled=True
    )
    grad_w1, grad_b1, grad_w2, grad_b2 = pl.pallas_call(
        functools.partial(split_kernel, ch),
        out_shape=(
            jax.ShapeDtypeStruct((3, 3, ch, ch), F32),
            jax.ShapeDtypeStruct((8, ch), F32),
            jax.ShapeDtypeStruct((3, 3, ch, ch), F32),
            jax.ShapeDtypeStruct((8, ch), F32),
        ),
        in_specs=[vmem],
        out_specs=(vmem,) * 4,
        name="split",
    )(full)
    return (back[None], grad_w1, grad_b1[0], grad_w2, grad_b2[0])


def solution(mesh):
    in_specs = (
        P("dp", "space", None, None),
        P("dp", "space", None, None),
        P("dp", None),
        P(),
        P(),
        P(),
        P(),
    )
    out_specs = (P("dp", "space", None, None), P(), P(), P(), P())
    return jax.shard_map(shards, mesh=mesh, in_specs=in_specs, out_specs=out_specs, check_vma=False)
```

```python
import functools
import math

import jax
import jax.numpy as jnp
from jax import lax
from jax.experimental import pallas as pl
from jax.experimental.pallas import tpu as pltpu
from jax.sharding import PartitionSpec as P

BF = jnp.bfloat16
F32 = jnp.float32
AXES = ("dp", "space")
FEAT_HALO = 4
GOAL_HALO = 2
GELU_SCALE = math.sqrt(2.0 / math.pi)
GELU_CUBE = 0.044715


def to_right(value):
    lane = lax.broadcasted_iota(jnp.int32, value.shape, 1)
    return jnp.where(lane == 0, jnp.zeros_like(value), pltpu.roll(value, 1, 1))


def to_left(value):
    last = value.shape[1] - 1
    lane = lax.broadcasted_iota(jnp.int32, value.shape, 1)
    return jnp.where(lane == last, jnp.zeros_like(value), pltpu.roll(value, last, 1))


def keep(flag, value):
    return jnp.where(flag > 0, value, jnp.zeros_like(value))


def masked(value, low, high):
    if low is None and high is None:
        return value
    half = value.shape[0] // 2
    first, second = value[:half], value[half:]
    if low is not None:
        first = keep(low, first)
    if high is not None:
        second = keep(high, second)
    return jnp.concatenate([first, second], axis=0)


def lane_sum(value):
    half = value.shape[0] // 2
    both = value[:half] + value[half:]
    total = both[:, :128]
    for start in range(128, both.shape[1], 128):
        total = total + both[:, start : start + 128]
    return total


def wave(position, channel):
    period = jnp.left_shift(jnp.full_like(channel, 4), channel & 7)
    phase = (position & (period - 1)).astype(F32)
    return jnp.sin(phase * ((2.0 * math.pi) / period.astype(F32)))


def row_waves(anchors_ref, start, half):
    shape = (half, 128)
    lane = lax.broadcasted_iota(jnp.int32, shape, 1)
    channel = lax.broadcasted_iota(jnp.int32, shape, 0)
    return wave(anchors_ref[0, 0] + start + lane, channel)


def col_waves(anchors_ref, half, cols):
    shape = (half, cols)
    lane = lax.broadcasted_iota(jnp.int32, shape, 1)
    channel = lax.broadcasted_iota(jnp.int32, shape, 0)
    return wave(anchors_ref[0, 1] + lane, channel)


def with_geo(value, row_wave, col_wave):
    rows = jnp.broadcast_to(row_wave, col_wave.shape)
    return value.astype(F32) + jnp.concatenate([rows, col_wave], axis=0)


def bias_tile(bias_ref):
    ch = bias_ref.shape[1]
    tile = jnp.transpose(jnp.broadcast_to(bias_ref[...], (128, ch)))
    return jnp.concatenate([tile, tile], axis=0)


def spread(matrix, block, mirrored=False):
    parts = jnp.dot(matrix, block, preferred_element_type=F32)
    pair = parts.shape[0] // 3
    left, right = (to_left, to_right) if mirrored else (to_right, to_left)
    return parts[pair : 2 * pair] + left(parts[:pair]) + right(parts[2 * pair :])


def activate(pre):
    square = pre * pre
    bent = jnp.tanh(pre * (GELU_SCALE + (GELU_SCALE * GELU_CUBE) * square))
    cdf = 0.5 + 0.5 * bent
    inner = GELU_SCALE + (3.0 * GELU_SCALE * GELU_CUBE) * square
    return pre * cdf, cdf + (0.5 * pre) * ((1.0 - bent * bent) * inner)


class Stage:
    def __init__(self, ch, cols):
        self.ch, self.cols = ch, cols

    def rows(self, at, count):
        return slice(at * self.ch, (at + count) * self.ch)

    def wide(self, tile):
        return jnp.tile(tile, (1, self.cols // 128))

    def put_three(self, target, at, value):
        spot = self.rows(at, 2)
        target[0, spot] = to_left(value)
        target[1, spot] = value
        target[2, spot] = to_right(value)

    def forward_one(self, matrix, bias, first, at, hidden, to, deriv=None, d_to=0, low=None, high=None):
        pre = spread(matrix[...], first[self.rows(at, 4)]) + self.wide(bias)
        value, grad = activate(pre)
        hidden[self.rows(to, 2)] = masked(value, low, high).astype(BF)
        if deriv is not None:
            deriv[self.rows(d_to, 2)] = grad

    def forward_two(self, matrix, bias, hidden, at, goal, misfit, to, total, flag=None):
        out = spread(matrix[...], hidden[self.rows(at, 4)]) + self.wide(bias)
        error = out - goal.astype(F32)
        if flag is not None:
            error = keep(flag, error)
        error = error.astype(BF)
        self.put_three(misfit, to, error)
        if flag is None:
            total[...] += lane_sum(error.astype(F32))

    def back(self, matrix, source, at):
        spot = self.rows(at, 4)
        stack = jnp.concatenate([source[0, spot], source[1, spot], source[2, spot]], axis=0)
        return jnp.dot(matrix[...], stack, preferred_element_type=F32)

    def backward_two(self, matrix, misfit, at, deriv, d_at, slope, to, total, low=None, high=None):
        value = self.back(matrix, misfit, at) * deriv[self.rows(d_at, 2)]
        value = masked(value, low, high).astype(BF)
        self.put_three(slope, to, value)
        wide = value.astype(F32)
        ch = self.ch
        if low is not None:
            wide = jnp.concatenate([jnp.zeros_like(wide[:ch]), wide[ch:]], axis=0)
        if high is not None:
            wide = jnp.concatenate([wide[:ch], jnp.zeros_like(wide[ch:])], axis=0)
        total[...] += lane_sum(wide)

    def weight_grad(self, acc, errors, e_at, source, at):
        spot = self.rows(e_at, 2)
        stack = jnp.concatenate([errors[0, spot], errors[1, spot], errors[2, spot]], axis=0)
        acc[...] += lax.dot_general(
            stack,
            source[self.rows(at, 4)],
            (((1,), (1,)), ((), ())),
            preferred_element_type=F32,
        )


def banded(blocks):
    flat = jnp.concatenate(blocks, axis=1)
    gap = jnp.zeros(blocks[0].shape, flat.dtype)
    return jnp.concatenate(
        [jnp.concatenate([flat, gap], axis=1), jnp.concatenate([gap, flat], axis=1)], axis=0
    )


def forward_band(w_ref, j):
    return banded([w_ref[i, j].astype(F32) for i in range(3)]).astype(BF)


def backward_band(w_ref, j):
    return banded([jnp.transpose(w_ref[2 - i, j].astype(F32)) for i in range(3)]).astype(BF)


def inner_kernel(
    rows,
    anchors_ref,
    w1_ref,
    w2_ref,
    b1_ref,
    b2_ref,
    feat_hbm,
    goal_hbm,
    back_hbm,
    first_edge,
    hidden_edge,
    deriv_edge,
    misfit_edge,
    slope_edge,
    fwd1,
    fwd2,
    bwd2,
    bwd1_spread,
    biases,
    col_wave_ref,
    acc1,
    acc2,
    sum1,
    sum2,
    feat,
    goal,
    first,
    hidden,
    deriv,
    misfit,
    slope,
    bwd1,
    back,
    in_sems,
    out_sems,
):
    ch, cols = feat.shape[1:]
    half, pair = ch // 2, 2 * ch
    me = lax.axis_index("space")
    do = Stage(ch, cols)
    loads = [
        pltpu.make_async_copy(feat_hbm.at[k : k + 4], feat.at[k : k + 4], in_sems.at[k // 4])
        for k in range(0, rows, 4)
    ]
    goal_load = pltpu.make_async_copy(goal_hbm, goal, in_sems.at[rows // 4])
    for load in loads:
        load.start()
    goal_load.start()
    for j in range(3):
        spot = slice(pair * j, pair * (j + 1))
        fwd1[spot] = forward_band(w1_ref, j)
        fwd2[spot] = forward_band(w2_ref, j)
        band = backward_band(w1_ref, j)
        bwd1_spread[spot] = band
        bwd1[:, 4 * ch * j : 4 * ch * (j + 1)] = band
        bwd2[:, 4 * ch * j : 4 * ch * (j + 1)] = backward_band(w2_ref, j)
    biases[0] = bias_tile(b1_ref)
    biases[1] = bias_tile(b2_ref)
    row_wave = row_waves(anchors_ref, me * rows, half)
    col_wave_ref[...] = col_waves(anchors_ref, half, cols)
    for total in (acc1, acc2, sum1, sum2):
        total[...] = jnp.zeros_like(total)
    for row in range(rows):
        if row % 4 == 0:
            loads[row // 4].wait()
        first[do.rows(row, 1)] = with_geo(
            feat[row], row_wave[:, row : row + 1], col_wave_ref[...]
        ).astype(BF)
    sends = []

    def send(source, target):
        copy = pltpu.make_async_copy(source, target, out_sems.at[len(sends)])
        copy.start()
        sends.append(copy)

    send(first.at[do.rows(0, 5)], first_edge.at[0])
    send(first.at[do.rows(rows - 5, 5)], first_edge.at[1])
    for r in range(1, rows - 2, 2):
        do.forward_one(fwd1, biases[0], first, r - 1, hidden, r - 1, deriv, r - 1)
    for side, r in enumerate((1, rows - 3)):
        send(hidden.at[do.rows(r - 1, 2)], hidden_edge.at[side])
        send(deriv.at[do.rows(r - 1, 2)], deriv_edge.at[side])
    goal_load.wait()
    for r in range(2, rows - 3, 2):
        goals = jnp.concatenate([goal[r], goal[r + 1]], axis=0)
        do.forward_two(fwd2, biases[1], hidden, r - 2, goals, misfit, r - 2, sum2)
        do.weight_grad(acc2, misfit, r - 2, hidden, r - 2)
    for side, r in enumerate((2, rows - 4)):
        send(misfit.at[:, do.rows(r - 2, 2)], misfit_edge.at[side])
    for r in range(3, rows - 4, 2):
        do.backward_two(bwd2, misfit, r - 3, deriv, r - 1, slope, r - 3, sum1)
    for side, r in enumerate((3, rows - 5)):
        send(slope.at[:, do.rows(r - 3, 2)], slope_edge.at[side])
    for r in range(4, rows - 5, 2):
        do.weight_grad(acc1, slope, r - 3, first, r - 1)
        value = do.back(bwd1, slope, r - 4).astype(BF)
        back[r - 4] = value[:ch]
        back[r - 3] = value[ch:]
    send(back, back_hbm.at[4 : rows - 4])
    for copy in sends:
        copy.wait()


def edge_kernel(
    rows,
    size,
    factor,
    anchors_ref,
    fwd1,
    fwd2,
    bwd2,
    biases,
    col_wave_ref,
    old1,
    old2,
    old_sum1,
    old_sum2,
    goal_hbm,
    even_hbm,
    odd_hbm,
    first_edge,
    hidden_edge,
    deriv_edge,
    misfit_edge,
    slope_edge,
    grads_ref,
    slope_out,
    halo,
    goal,
    first,
    hidden,
    deriv,
    misfit,
    slope,
    acc1,
    acc2,
    sum1,
    sum2,
    halo_sems,
    in_sems,
    out_sems,
):
    ch, cols = goal.shape[2:]
    half = ch // 2
    me = lax.axis_index("space")
    above = (me > 0).astype(jnp.int32)
    below = (me < size - 1).astype(jnp.int32)
    odd = lax.rem(me, 2)
    do = Stage(ch, cols)
    for side in range(2):

        @pl.when(odd == side)
        def _():
            pltpu.make_async_copy(odd_hbm, halo.at[side], halo_sems.at[side]).start()

        @pl.when(odd != side)
        def _():
            pltpu.make_async_copy(even_hbm, halo.at[side], halo_sems.at[side]).start()

    places = (
        (first_edge, first, (4, 0), 5, False),
        (hidden_edge, hidden, (4, 0), 2, False),
        (deriv_edge, deriv, (2, 0), 2, False),
        (misfit_edge, misfit, (4, 0), 2, True),
        (slope_edge, slope, (4, 0), 2, True),
    )
    loads = []

    def load(source, target):
        copy = pltpu.make_async_copy(source, target, in_sems.at[len(loads)])
        copy.start()
        loads.append(copy)

    for source, target, spots, count, three in places:
        for side in range(2):
            spot = do.rows(spots[side], count)
            load(
                source.at[side],
                target.at[side, :, spot] if three else target.at[side, spot],
            )
    for side, r in enumerate((0, rows - 2)):
        load(goal_hbm.at[r : r + 2], goal.at[side])
    acc1[...] = old1[...]
    acc2[...] = old2[...]
    sum1[...] = old_sum1[...]
    sum2[...] = old_sum2[...]
    flags = (above, below)
    for side in range(2):
        pltpu.make_async_copy(even_hbm, halo.at[side], halo_sems.at[side]).wait()
    for side, (start, to) in enumerate(((-4, 0), (rows, 5))):
        row_wave = row_waves(anchors_ref, me * rows + start, half)
        for k in range(4):
            value = with_geo(halo[side, k], row_wave[:, k : k + 1], col_wave_ref[...])
            first[side, do.rows(to + k, 1)] = keep(flags[side], value).astype(BF)
    for copy in loads:
        copy.wait()
    top, low = 0, 1
    F, H, D, M, S = ([ref.at[0], ref.at[1]] for ref in (first, hidden, deriv, misfit, slope))
    one = functools.partial(do.forward_one, fwd1, biases[0])
    one(F[top], 0, H[top], 0, low=above, high=above)
    one(F[low], 5, H[low], 4, low=below, high=below)
    one(F[top], 2, H[top], 2, D[top], 0, low=above)
    one(F[low], 3, H[low], 2, D[low], 2, high=below)

    def goals(ref, side, at):
        return jnp.concatenate([ref[side, at], ref[side, at + 1]], axis=0)

    two = functools.partial(do.forward_two, fwd2, biases[1])
    two(H[top], 0, goals(halo, 0, 4), M[top], 0, sum2, flag=above)
    two(H[low], 2, goals(halo, 1, 4), M[low], 4, sum2, flag=below)
    two(H[top], 2, goals(goal, 0, 0), M[top], 2, sum2)
    two(H[low], 0, goals(goal, 1, 0), M[low], 2, sum2)
    do.weight_grad(acc2, M[top], 2, H[top], 2)
    do.weight_grad(acc2, M[low], 2, H[low], 0)
    bend = functools.partial(do.backward_two, bwd2)
    bend(M[top], 0, D[top], 0, S[top], 0, sum1, low=above)
    bend(M[low], 2, D[low], 2, S[low], 4, sum1, high=below)
    bend(M[top], 2, D[top], 2, S[top], 2, sum1)
    bend(M[low], 0, D[low], 0, S[low], 2, sum1)
    sends = [
        pltpu.make_async_copy(slope.at[side, 1], slope_out.at[side], out_sems.at[side])
        for side in range(2)
    ]
    for copy in sends:
        copy.start()
    do.weight_grad(acc1, S[top], 1, F[top], 3)
    do.weight_grad(acc1, S[low], 1, F[low], 0)
    do.weight_grad(acc1, S[top], 3, F[top], 5)
    do.weight_grad(acc1, S[low], 3, F[low], 2)

    def emit(base, acc, total):
        summed = jnp.sum(total[...], axis=1, keepdims=True)
        side = jnp.broadcast_to(summed, (ch, ch))
        for j in range(3):
            upper = acc[2 * j * ch : (2 * j + 1) * ch]
            lower = acc[(2 * j + 1) * ch : (2 * j + 2) * ch]
            block = jnp.concatenate([upper[:, : 3 * ch] + lower[:, ch:], side], axis=1) * factor
            for t in range(ch // 8):
                for part in range(2):
                    grads_ref[base + (j * (ch // 8) + t) * 2 + part] = block[
                        8 * t : 8 * t + 8, 128 * part : 128 * part + 128
                    ]

    emit(0, acc1, sum1)
    emit(6 * (ch // 8), acc2, sum2)
    for spare in range(12 * (ch // 8), grads_ref.shape[0]):
        grads_ref[spare] = jnp.zeros((8, 128), F32)
    for copy in sends:
        copy.wait()


def rest_kernel(rows, old_back, bwd1_spread, slope, back_hbm, back, sems):
    ch = back.shape[2]
    do = Stage(ch, back.shape[3])
    sends = []
    for at in range(2):
        for side in range(2):
            block = slope[side, do.rows(2 * at, 4)]
            value = spread(bwd1_spread[...], block, mirrored=True).astype(BF)
            back[side, 2 * at] = value[:ch]
            back[side, 2 * at + 1] = value[ch:]
    for side, r in enumerate((0, rows - 4)):
        copy = pltpu.make_async_copy(back.at[side], back_hbm.at[r : r + 4], sems.at[side])
        copy.start()
        sends.append(copy)
    for copy in sends:
        copy.wait()


def split_kernel(ch, full_ref, w1_ref, b1_ref, w2_ref, b2_ref):
    for base, w_ref, b_ref in ((0, w1_ref, b1_ref), (6 * (ch // 8), w2_ref, b2_ref)):
        for j in range(3):
            left, right = [
                jnp.concatenate(
                    [
                        full_ref[base + (j * (ch // 8) + t) * 2 + part].astype(F32)
                        for t in range(ch // 8)
                    ],
                    axis=0,
                )
                for part in range(2)
            ]
            w_ref[0, j] = left[:, :ch]
            w_ref[1, j] = left[:, ch:]
            w_ref[2, j] = right[:, :ch]
            if j == 0:
                b_ref[...] = jnp.transpose(right)[ch : ch + 1]


def shards(features, target, anchors, w_first, b_first, w_second, b_second):
    _, rows, ch, cols = features.shape
    size = lax.axis_size("space")
    devices = size * lax.axis_size("dp")
    me = lax.axis_index("space")
    factor = 1.0 / math.sqrt(features.shape[0] * devices * rows * cols)
    feats, goals = features[0], target[0]
    pair, quad = 2 * ch, 4 * ch

    def edge(wants_bottom):
        start = jnp.where(wants_bottom, rows - FEAT_HALO, 0)
        goal_start = jnp.where(wants_bottom, rows - GOAL_HALO, 0)
        return jnp.concatenate(
            [
                lax.dynamic_slice_in_dim(feats, start, FEAT_HALO),
                lax.dynamic_slice_in_dim(goals, goal_start, GOAL_HALO),
            ]
        )

    is_even = lax.rem(me, 2) == 0
    links = [
        [
            link
            for low in range(first, size - 1, 2)
            for link in ((low, low + 1), (low + 1, low))
        ]
        for first in (0, 1)
    ]
    even_halo = lax.ppermute(edge(is_even), "space", links[0])
    odd_halo = lax.ppermute(edge(jnp.logical_not(is_even)), "space", links[1])

    vmem = pl.BlockSpec(memory_space=pltpu.VMEM)
    smem = pl.BlockSpec(memory_space=pltpu.SMEM)
    anywhere = pl.BlockSpec(memory_space=pl.ANY)

    def shape(*dims, dtype=BF):
        return jax.ShapeDtypeStruct(dims, dtype)

    def buffer(count, *lead, dtype=BF):
        return pltpu.VMEM(lead + (count * ch, cols), dtype)

    (
        back,
        first_edge,
        hidden_edge,
        deriv_edge,
        misfit_edge,
        slope_edge,
        fwd1,
        fwd2,
        bwd2,
        bwd1_spread,
        biases,
        col_wave,
        acc1,
        acc2,
        sum1,
        sum2,
    ) = pl.pallas_call(
        functools.partial(inner_kernel, rows),
        out_shape=(
            shape(rows, ch, cols),
            shape(2, 5 * ch, cols),
            shape(2, pair, cols),
            shape(2, pair, cols, dtype=F32),
            shape(2, 3, pair, cols),
            shape(2, 3, pair, cols),
            shape(3 * pair, quad),
            shape(3 * pair, quad),
            shape(pair, 3 * quad),
            shape(3 * pair, quad),
            shape(2, pair, 128, dtype=F32),
            shape(ch // 2, cols, dtype=F32),
            shape(3 * pair, quad, dtype=F32),
            shape(3 * pair, quad, dtype=F32),
            shape(ch, 128, dtype=F32),
            shape(ch, 128, dtype=F32),
        ),
        in_specs=[smem] + [vmem] * 4 + [anywhere] * 2,
        out_specs=(anywhere,) * 6 + (vmem,) * 10,
        scratch_shapes=[
            pltpu.VMEM((rows, ch, cols), BF),
            pltpu.VMEM((rows, ch, cols), BF),
            buffer(rows),
            buffer(rows - 2),
            buffer(rows - 2, dtype=F32),
            buffer(rows - 4, 3),
            buffer(rows - 6, 3),
            pltpu.VMEM((pair, 3 * quad), BF),
            pltpu.VMEM((rows - 8, ch, cols), BF),
            pltpu.SemaphoreType.DMA((rows // 4 + 1,)),
            pltpu.SemaphoreType.DMA((11,)),
        ],
        compiler_params=pltpu.CompilerParams(vmem_limit_bytes=40 << 20),
        cost_estimate=pl.CostEstimate(
            flops=14 * 10**9, bytes_accessed=12 * 10**6, transcendentals=10**6
        ),
        name="inner",
    )(
        anchors,
        w_first,
        w_second,
        b_first[None],
        b_second[None],
        feats,
        goals,
    )
    grads, slope = pl.pallas_call(
        functools.partial(edge_kernel, rows, size, factor),
        out_shape=(shape(devices, 8, 128, dtype=F32), shape(2, 6 * ch, cols)),
        in_specs=[smem] + [vmem] * 9 + [anywhere] * 8,
        out_specs=(vmem, anywhere),
        scratch_shapes=[
            pltpu.VMEM((2, FEAT_HALO + GOAL_HALO, ch, cols), BF),
            pltpu.VMEM((2, GOAL_HALO, ch, cols), BF),
            buffer(9, 2),
            buffer(6, 2),
            buffer(4, 2, dtype=F32),
            buffer(6, 2, 3),
            buffer(6, 2, 3),
            pltpu.VMEM((3 * pair, quad), F32),
            pltpu.VMEM((3 * pair, quad), F32),
            pltpu.VMEM((ch, 128), F32),
            pltpu.VMEM((ch, 128), F32),
            pltpu.SemaphoreType.DMA((2,)),
            pltpu.SemaphoreType.DMA((12,)),
            pltpu.SemaphoreType.DMA((2,)),
        ],
        compiler_params=pltpu.CompilerParams(vmem_limit_bytes=40 << 20),
        cost_estimate=pl.CostEstimate(
            flops=9 * 10**9, bytes_accessed=10 * 10**6, transcendentals=5 * 10**5
        ),
        name="edges",
    )(
        anchors,
        fwd1,
        fwd2,
        bwd2,
        biases,
        col_wave,
        acc1,
        acc2,
        sum1,
        sum2,
        goals,
        even_halo,
        odd_halo,
        first_edge,
        hidden_edge,
        deriv_edge,
        misfit_edge,
        slope_edge,
    )
    parts = lax.all_to_all(grads, AXES, 0, 0, tiled=True)
    back = pl.pallas_call(
        functools.partial(rest_kernel, rows),
        out_shape=shape(rows, ch, cols),
        in_specs=[anywhere, vmem, vmem],
        out_specs=anywhere,
        scratch_shapes=[
            pltpu.VMEM((2, 4, ch, cols), BF),
            pltpu.SemaphoreType.DMA((2,)),
        ],
        input_output_aliases={0: 0},
        compiler_params=pltpu.CompilerParams(vmem_limit_bytes=20 << 20),
        cost_estimate=pl.CostEstimate(
            flops=2 * 10**9, bytes_accessed=3 * 10**6, transcendentals=0
        ),
        name="rest",
    )(back, bwd1_spread, slope)
    mine = jnp.sum(parts, axis=0).astype(BF)
    full = lax.all_to_all(
        jnp.broadcast_to(mine[None], (devices, 8, 128)), AXES, 0, 0, tiled=True
    )
    grad_w1, grad_b1, grad_w2, grad_b2 = pl.pallas_call(
        functools.partial(split_kernel, ch),
        out_shape=(
            shape(3, 3, ch, ch, dtype=F32),
            shape(1, ch, dtype=F32),
            shape(3, 3, ch, ch, dtype=F32),
            shape(1, ch, dtype=F32),
        ),
        in_specs=[vmem],
        out_specs=(vmem,) * 4,
        name="split",
    )(full)
    return (back[None], grad_w1, grad_b1[0], grad_w2, grad_b2[0])


def solution(mesh):
    in_specs = (
        P("dp", "space", None, None),
        P("dp", "space", None, None),
        P("dp", None),
        P(),
        P(),
        P(),
        P(),
    )
    out_specs = (P("dp", "space", None, None), P(), P(), P(), P())
    return jax.shard_map(shards, mesh=mesh, in_specs=in_specs, out_specs=out_specs, check_vma=False)
```

```python
import functools
import math

import jax
import jax.numpy as jnp
from jax import lax
from jax.experimental import pallas as pl
from jax.experimental.pallas import tpu as pltpu
from jax.sharding import PartitionSpec as P

BF = jnp.bfloat16
F32 = jnp.float32
AXES = ("dp", "space")
FEAT_HALO = 4
GOAL_HALO = 2
GELU_SCALE = math.sqrt(2.0 / math.pi)
GELU_CUBE = 0.044715


def to_right(value):
    moved = pltpu.roll(value, 1, 1)
    edge = moved[:, :128]
    lane = lax.broadcasted_iota(jnp.int32, edge.shape, 1)
    edge = jnp.where(lane == 0, jnp.zeros_like(edge), edge)
    return jnp.concatenate([edge, moved[:, 128:]], axis=1)


def to_left(value):
    cols = value.shape[1]
    moved = pltpu.roll(value, cols - 1, 1)
    edge = moved[:, cols - 128 :]
    lane = lax.broadcasted_iota(jnp.int32, edge.shape, 1)
    edge = jnp.where(lane == 127, jnp.zeros_like(edge), edge)
    return jnp.concatenate([moved[:, : cols - 128], edge], axis=1)


def keep(flag, value):
    return jnp.where(flag > 0, value, jnp.zeros_like(value))


def masked(value, low, high):
    if low is None and high is None:
        return value
    half = value.shape[0] // 2
    first, second = value[:half], value[half:]
    if low is not None:
        first = keep(low, first)
    if high is not None:
        second = keep(high, second)
    return jnp.concatenate([first, second], axis=0)


def lane_sum(value):
    half = value.shape[0] // 2
    both = value[:half] + value[half:]
    total = both[:, :128]
    for start in range(128, both.shape[1], 128):
        total = total + both[:, start : start + 128]
    return total


def wave(position, channel):
    period = jnp.left_shift(jnp.full_like(channel, 4), channel & 7)
    phase = (position & (period - 1)).astype(F32)
    return jnp.sin(phase * ((2.0 * math.pi) / period.astype(F32)))


def row_waves(anchors_ref, start, half):
    shape = (half, 128)
    lane = lax.broadcasted_iota(jnp.int32, shape, 1)
    channel = lax.broadcasted_iota(jnp.int32, shape, 0)
    return wave(anchors_ref[0, 0] + start + lane, channel)


def col_waves(anchors_ref, half, cols):
    shape = (half, cols)
    lane = lax.broadcasted_iota(jnp.int32, shape, 1)
    channel = lax.broadcasted_iota(jnp.int32, shape, 0)
    return wave(anchors_ref[0, 1] + lane, channel)


def with_geo(value, row_wave, col_wave):
    rows = jnp.broadcast_to(row_wave, col_wave.shape)
    return value.astype(F32) + jnp.concatenate([rows, col_wave], axis=0)


def bias_tile(bias_ref):
    ch = bias_ref.shape[1]
    tile = jnp.transpose(jnp.broadcast_to(bias_ref[...], (128, ch)))
    return jnp.concatenate([tile, tile], axis=0)


def spread(matrix, block, mirrored=False):
    parts = jnp.dot(matrix, block, preferred_element_type=F32)
    pair = parts.shape[0] // 3
    left, right = (to_left, to_right) if mirrored else (to_right, to_left)
    return parts[pair : 2 * pair] + left(parts[:pair]) + right(parts[2 * pair :])


def activate(pre):
    square = pre * pre
    cdf = 0.5 + 0.5 * jnp.tanh(pre * (GELU_SCALE + (GELU_SCALE * GELU_CUBE) * square))
    value = pre * cdf
    bend = 2.0 * GELU_SCALE + (6.0 * GELU_SCALE * GELU_CUBE) * square
    return value, cdf + value * ((1.0 - cdf) * bend)


def view(*parts):
    def read(at, count, ch, plane=None):
        blocks = []
        for ref, start, rows in parts:
            low, high = max(at, 0), min(at + count, rows)
            if low < high:
                spot = slice((start + low) * ch, (start + high) * ch)
                blocks.append(ref[spot] if plane is None else ref[plane, spot])
            at, count = at - rows, count
        return blocks[0] if len(blocks) == 1 else jnp.concatenate(blocks, axis=0)

    return read


class Stage:
    def __init__(self, ch, cols):
        self.ch, self.cols = ch, cols

    def rows(self, at, count):
        return slice(at * self.ch, (at + count) * self.ch)

    def wide(self, tile):
        return jnp.tile(tile, (1, self.cols // 128))

    def put_three(self, target, at, value):
        spot = self.rows(at, 2)
        target[0, spot] = to_left(value)
        target[1, spot] = value
        target[2, spot] = to_right(value)

    def forward_one(self, matrix, bias, first, at, hidden, to, deriv=None, d_to=0, low=None, high=None):
        pre = spread(matrix[...], first(at, 4, self.ch)) + self.wide(bias)
        value, grad = activate(pre)
        hidden[self.rows(to, 2)] = masked(value, low, high).astype(BF)
        if deriv is not None:
            deriv[self.rows(d_to, 2)] = grad

    def forward_two(self, matrix, bias, hidden, at, goal, misfit, to, total, flag=None):
        out = spread(matrix[...], hidden(at, 4, self.ch)) + self.wide(bias)
        error = out - goal.astype(F32)
        if flag is not None:
            error = keep(flag, error)
        error = error.astype(BF)
        self.put_three(misfit, to, error)
        if flag is None:
            total[...] += lane_sum(error.astype(F32))

    def three(self, source, at, count):
        return jnp.concatenate([source(at, count, self.ch, plane) for plane in range(3)], axis=0)

    def back(self, matrix, source, at):
        return jnp.dot(matrix[...], self.three(source, at, 4), preferred_element_type=F32)

    def backward_two(self, matrix, misfit, at, deriv, d_at, slope, to, total, low=None, high=None):
        value = self.back(matrix, misfit, at) * deriv(d_at, 2, self.ch)
        value = masked(value, low, high).astype(BF)
        self.put_three(slope, to, value)
        wide = value.astype(F32)
        ch = self.ch
        if low is not None:
            wide = jnp.concatenate([jnp.zeros_like(wide[:ch]), wide[ch:]], axis=0)
        if high is not None:
            wide = jnp.concatenate([wide[:ch], jnp.zeros_like(wide[ch:])], axis=0)
        total[...] += lane_sum(wide)

    def weight_grad(self, acc, errors, e_at, source, at):
        acc[...] += lax.dot_general(
            self.three(errors, e_at, 2),
            source(at, 4, self.ch),
            (((1,), (1,)), ((), ())),
            preferred_element_type=F32,
        )


def banded(blocks):
    flat = jnp.concatenate(blocks, axis=1)
    gap = jnp.zeros(blocks[0].shape, flat.dtype)
    return jnp.concatenate(
        [jnp.concatenate([flat, gap], axis=1), jnp.concatenate([gap, flat], axis=1)], axis=0
    )


def forward_band(w_ref, j):
    return banded([w_ref[i, j].astype(F32) for i in range(3)]).astype(BF)


def backward_band(w_ref, j):
    return banded([jnp.transpose(w_ref[2 - i, j].astype(F32)) for i in range(3)]).astype(BF)


def pack_kernel(rows, feat_hbm, goal_hbm, w1_hbm, w2_hbm, even_ref, odd_ref, w1_ref, w2_ref, sems):
    odd = lax.rem(lax.axis_index("space"), 2)
    copies = []

    def start(source, target):
        copies.append(pltpu.make_async_copy(source, target, sems.at[len(copies)]))
        copies[-1].start()

    for which, ref in enumerate((even_ref, odd_ref)):
        bottom = jnp.where(odd == which, 1, 0)
        for source, count, at in ((feat_hbm, FEAT_HALO, 0), (goal_hbm, GOAL_HALO, FEAT_HALO)):
            start(source.at[pl.ds(bottom * (rows - count), count)], ref.at[at : at + count])
    start(w1_hbm, w1_ref)
    start(w2_hbm, w2_ref)
    for copy in copies:
        copy.wait()


def inner_kernel(
    rows,
    anchors_ref,
    w1_ref,
    w2_ref,
    b1_ref,
    b2_ref,
    feat,
    goal,
    back_hbm,
    first,
    hidden,
    deriv,
    misfit,
    slope,
    fwd1,
    fwd2,
    bwd2,
    bwd1_spread,
    biases,
    col_wave_ref,
    acc1,
    acc2,
    sum1,
    sum2,
    bwd1,
    back,
    sem,
):
    ch, cols = feat.shape[1:]
    half, pair = ch // 2, 2 * ch
    me = lax.axis_index("space")
    do = Stage(ch, cols)
    for j in range(3):
        spot = slice(pair * j, pair * (j + 1))
        fwd1[spot] = forward_band(w1_ref, j)
        fwd2[spot] = forward_band(w2_ref, j)
        band = backward_band(w1_ref, j)
        bwd1_spread[spot] = band
        bwd1[:, 4 * ch * j : 4 * ch * (j + 1)] = band
        bwd2[:, 4 * ch * j : 4 * ch * (j + 1)] = backward_band(w2_ref, j)
    biases[0] = bias_tile(b1_ref)
    biases[1] = bias_tile(b2_ref)
    row_wave = row_waves(anchors_ref, me * rows, half)
    col_wave_ref[...] = col_waves(anchors_ref, half, cols)
    for total in (acc1, acc2, sum1, sum2):
        total[...] = jnp.zeros_like(total)
    for row in range(rows):
        first[do.rows(row, 1)] = with_geo(
            feat[row], row_wave[:, row : row + 1], col_wave_ref[...]
        ).astype(BF)
    F, H, D = view((first, 0, rows)), view((hidden, 0, rows - 2)), view((deriv, 0, rows - 2))
    M, S = view((misfit, 0, rows - 4)), view((slope, 0, rows - 6))

    def conv_one(r):
        do.forward_one(fwd1, biases[0], F, r - 1, hidden, r - 1, deriv, r - 1)

    def conv_two(r):
        goals = jnp.concatenate([goal[r], goal[r + 1]], axis=0)
        do.forward_two(fwd2, biases[1], H, r - 2, goals, misfit, r - 2, sum2)

    def grad_two(r):
        do.weight_grad(acc2, M, r - 2, H, r - 2)

    def bend(r):
        do.backward_two(bwd2, M, r - 3, D, r - 1, slope, r - 3, sum1)

    def grad_one(r):
        do.weight_grad(acc1, S, r - 3, F, r - 1)

    def input_grad(r):
        value = do.back(bwd1, S, r - 4).astype(BF)
        back[r - 4] = value[:ch]
        back[r - 3] = value[ch:]

    steps = (
        (grad_one, 4, rows - 6, 6),
        (input_grad, 4, rows - 6, 6),
        (bend, 3, rows - 5, 4),
        (grad_two, 2, rows - 4, 3),
        (conv_two, 2, rows - 4, 2),
        (conv_one, 1, rows - 3, 0),
    )
    for turn in range(rows // 2 + 3):
        for step, low, high, lag in steps:
            r = low + 2 * (turn - lag)
            if low <= r <= high:
                step(r)
    copy = pltpu.make_async_copy(back, back_hbm.at[4 : rows - 4], sem)
    copy.start()
    copy.wait()


def edge_kernel(
    rows,
    size,
    factor,
    anchors_ref,
    fwd1,
    fwd2,
    bwd2,
    biases,
    col_wave_ref,
    old1,
    old2,
    old_sum1,
    old_sum2,
    goal,
    even_halo,
    odd_halo,
    first,
    hidden,
    deriv,
    misfit,
    slope,
    grads_ref,
    slope_out,
    new_first,
    new_hidden,
    new_deriv,
    new_misfit,
    new_slope,
    acc1,
    acc2,
    sum1,
    sum2,
):
    ch, cols = goal.shape[1:]
    half = ch // 2
    me = lax.axis_index("space")
    above = (me > 0).astype(jnp.int32)
    below = (me < size - 1).astype(jnp.int32)
    odd = lax.rem(me, 2)
    do = Stage(ch, cols)
    flags = (above, below)

    def halo(side, k):
        return jnp.where(odd == side, odd_halo[k], even_halo[k])

    acc1[...] = old1[...]
    acc2[...] = old2[...]
    sum1[...] = old_sum1[...]
    sum2[...] = old_sum2[...]
    for side, start in enumerate((-4, rows)):
        row_wave = row_waves(anchors_ref, me * rows + start, half)
        for k in range(4):
            value = with_geo(halo(side, k), row_wave[:, k : k + 1], col_wave_ref[...])
            new_first[side, do.rows(k, 1)] = keep(flags[side], value).astype(BF)
    top, low = 0, 1
    nF, nH, nD, nM, nS = (
        [ref.at[0], ref.at[1]] for ref in (new_first, new_hidden, new_deriv, new_misfit, new_slope)
    )
    F = (view((nF[top], 0, 4), (first, 0, 5)), view((first, rows - 5, 5), (nF[low], 0, 4)))
    H = (view((nH[top], 0, 4), (hidden, 0, 2)), view((hidden, rows - 4, 2), (nH[low], 0, 4)))
    D = (view((nD[top], 0, 2), (deriv, 0, 2)), view((deriv, rows - 4, 2), (nD[low], 0, 2)))
    M = (view((nM[top], 0, 4), (misfit, 0, 2)), view((misfit, rows - 6, 2), (nM[low], 0, 4)))
    S = (view((nS[top], 0, 4), (slope, 0, 2)), view((slope, rows - 8, 2), (nS[low], 0, 4)))
    one = functools.partial(do.forward_one, fwd1, biases[0])
    one(F[top], 2, nH[top], 2, nD[top], 0, low=above)
    one(F[low], 3, nH[low], 0, nD[low], 0, high=below)
    one(F[top], 0, nH[top], 0, low=above, high=above)
    one(F[low], 5, nH[low], 2, low=below, high=below)
    two = functools.partial(do.forward_two, fwd2, biases[1])
    two(H[top], 2, jnp.concatenate([goal[0], goal[1]], axis=0), nM[top], 2, sum2)
    two(
        H[low], 0, jnp.concatenate([goal[rows - 2], goal[rows - 1]], axis=0), nM[low], 0, sum2
    )
    two(H[top], 0, jnp.concatenate([halo(0, 4), halo(0, 5)], axis=0), nM[top], 0, sum2, above)
    two(H[low], 2, jnp.concatenate([halo(1, 4), halo(1, 5)], axis=0), nM[low], 2, sum2, below)
    bend = functools.partial(do.backward_two, bwd2)
    bend(M[top], 2, D[top], 2, nS[top], 2, sum1)
    bend(M[low], 0, D[low], 0, nS[low], 0, sum1)
    do.weight_grad(acc2, M[top], 2, H[top], 2)
    bend(M[top], 0, D[top], 0, nS[top], 0, sum1, low=above)
    bend(M[low], 2, D[low], 2, nS[low], 2, sum1, high=below)
    do.weight_grad(acc2, M[low], 2, H[low], 0)
    do.weight_grad(acc1, S[top], 3, F[top], 5)
    do.weight_grad(acc1, S[low], 1, F[low], 0)
    do.weight_grad(acc1, S[top], 1, F[top], 3)
    do.weight_grad(acc1, S[low], 3, F[low], 2)
    slope_out[...] = new_slope[:, 1]

    def emit(base, acc, total):
        summed = jnp.sum(total[...], axis=1, keepdims=True)
        side = jnp.broadcast_to(summed, (ch, ch))
        for j in range(3):
            upper = acc[2 * j * ch : (2 * j + 1) * ch]
            lower = acc[(2 * j + 1) * ch : (2 * j + 2) * ch]
            block = jnp.concatenate([upper[:, : 3 * ch] + lower[:, ch:], side], axis=1) * factor
            for t in range(ch // 8):
                for part in range(2):
                    grads_ref[base + (j * (ch // 8) + t) * 2 + part] = block[
                        8 * t : 8 * t + 8, 128 * part : 128 * part + 128
                    ]

    emit(0, acc1, sum1)
    emit(6 * (ch // 8), acc2, sum2)
    for spare in range(12 * (ch // 8), grads_ref.shape[0]):
        grads_ref[spare] = jnp.zeros((8, 128), F32)


def rest_kernel(rows, old_back, bwd1_spread, new_slope, slope, back_hbm, back, sems):
    ch = back.shape[2]
    do = Stage(ch, back.shape[3])
    inside = slope.at[1]
    S = (
        view((new_slope.at[0], 0, 4), (inside, 0, 2)),
        view((inside, rows - 8, 2), (new_slope.at[1], 0, 4)),
    )
    copies = []
    for side, r in enumerate((0, rows - 4)):
        for at in range(2):
            value = spread(bwd1_spread[...], S[side](2 * at, 4, ch), mirrored=True).astype(BF)
            back[side, 2 * at] = value[:ch]
            back[side, 2 * at + 1] = value[ch:]
        copy = pltpu.make_async_copy(back.at[side], back_hbm.at[r : r + 4], sems.at[side])
        copy.start()
        copies.append(copy)
    for copy in copies:
        copy.wait()


def sum_kernel(parts_ref, out_ref):
    total = jnp.sum(parts_ref[...], axis=0).astype(BF)
    out_ref[...] = jnp.broadcast_to(total[None], out_ref.shape)


def split_kernel(ch, full_ref, w1_ref, b1_ref, w2_ref, b2_ref):
    for base, w_ref, b_ref in ((0, w1_ref, b1_ref), (6 * (ch // 8), w2_ref, b2_ref)):
        for j in range(3):
            left, right = [
                jnp.concatenate(
                    [
                        full_ref[base + (j * (ch // 8) + t) * 2 + part].astype(F32)
                        for t in range(ch // 8)
                    ],
                    axis=0,
                )
                for part in range(2)
            ]
            w_ref[0, j] = left[:, :ch]
            w_ref[1, j] = left[:, ch:]
            w_ref[2, j] = right[:, :ch]
            if j == 0:
                b_ref[...] = jnp.transpose(right)[ch : ch + 1]


def shards(features, target, anchors, w_first, b_first, w_second, b_second):
    _, rows, ch, cols = features.shape
    size = lax.axis_size("space")
    devices = size * lax.axis_size("dp")
    factor = 1.0 / math.sqrt(features.shape[0] * devices * rows * cols)
    feats, goals = features[0], target[0]
    pair, quad = 2 * ch, 4 * ch

    links = [
        [
            link
            for low in range(first, size - 1, 2)
            for link in ((low, low + 1), (low + 1, low))
        ]
        for first in (0, 1)
    ]
    vmem = pl.BlockSpec(memory_space=pltpu.VMEM)
    smem = pl.BlockSpec(memory_space=pltpu.SMEM)
    hbm = pl.BlockSpec(memory_space=pltpu.HBM)

    def shape(*dims, dtype=BF):
        return jax.ShapeDtypeStruct(dims, dtype)

    def buffer(count, *lead, dtype=BF):
        return pltpu.VMEM(lead + (count * ch, cols), dtype)

    even_edge, odd_edge, w_first, w_second = pl.pallas_call(
        functools.partial(pack_kernel, rows),
        out_shape=(shape(FEAT_HALO + GOAL_HALO, ch, cols),) * 2 + (shape(3, 3, ch, ch),) * 2,
        in_specs=[hbm] * 4,
        out_specs=(vmem,) * 4,
        scratch_shapes=[pltpu.SemaphoreType.DMA((6,))],
        compiler_params=pltpu.CompilerParams(vmem_limit_bytes=8 << 20),
        name="pack",
    )(
        *(
            pltpu.with_memory_space_constraint(array, pltpu.HBM)
            for array in (feats, goals, w_first, w_second)
        )
    )
    odd_halo = lax.ppermute(odd_edge, "space", links[1])
    even_halo = lax.ppermute(even_edge, "space", links[0])
    (
        back,
        first,
        hidden,
        deriv,
        misfit,
        slope,
        fwd1,
        fwd2,
        bwd2,
        bwd1_spread,
        biases,
        col_wave,
        acc1,
        acc2,
        sum1,
        sum2,
    ) = pl.pallas_call(
        functools.partial(inner_kernel, rows),
        out_shape=(
            shape(rows, ch, cols),
            shape(rows * ch, cols),
            shape((rows - 2) * ch, cols),
            shape((rows - 2) * ch, cols, dtype=F32),
            shape(3, (rows - 4) * ch, cols),
            shape(3, (rows - 6) * ch, cols),
            shape(3 * pair, quad),
            shape(3 * pair, quad),
            shape(pair, 3 * quad),
            shape(3 * pair, quad),
            shape(2, pair, 128, dtype=F32),
            shape(ch // 2, cols, dtype=F32),
            shape(3 * pair, quad, dtype=F32),
            shape(3 * pair, quad, dtype=F32),
            shape(ch, 128, dtype=F32),
            shape(ch, 128, dtype=F32),
        ),
        in_specs=[smem] + [vmem] * 6,
        out_specs=(hbm,) + (vmem,) * 15,
        scratch_shapes=[
            pltpu.VMEM((pair, 3 * quad), BF),
            pltpu.VMEM((rows - 8, ch, cols), BF),
            pltpu.SemaphoreType.DMA,
        ],
        compiler_params=pltpu.CompilerParams(vmem_limit_bytes=24 << 20),
        cost_estimate=pl.CostEstimate(
            flops=14 * 10**9, bytes_accessed=12 * 10**6, transcendentals=10**6
        ),
        name="inner",
    )(
        anchors,
        w_first,
        w_second,
        b_first[None],
        b_second[None],
        feats,
        goals,
    )
    grads, new_slope = pl.pallas_call(
        functools.partial(edge_kernel, rows, size, factor),
        out_shape=(shape(devices, 8, 128, dtype=F32), shape(2, 4 * ch, cols)),
        in_specs=[smem] + [vmem] * 17,
        out_specs=(vmem,) * 2,
        scratch_shapes=[
            buffer(4, 2),
            buffer(4, 2),
            buffer(2, 2, dtype=F32),
            buffer(4, 2, 3),
            buffer(4, 2, 3),
            pltpu.VMEM((3 * pair, quad), F32),
            pltpu.VMEM((3 * pair, quad), F32),
            pltpu.VMEM((ch, 128), F32),
            pltpu.VMEM((ch, 128), F32),
        ],
        compiler_params=pltpu.CompilerParams(vmem_limit_bytes=24 << 20),
        cost_estimate=pl.CostEstimate(
            flops=9 * 10**9, bytes_accessed=10 * 10**6, transcendentals=5 * 10**5
        ),
        name="edges",
    )(
        anchors,
        fwd1,
        fwd2,
        bwd2,
        biases,
        col_wave,
        acc1,
        acc2,
        sum1,
        sum2,
        goals,
        even_halo,
        odd_halo,
        first,
        hidden,
        deriv,
        misfit,
        slope,
    )
    parts = lax.all_to_all(grads, AXES, 0, 0, tiled=True)
    back = pl.pallas_call(
        functools.partial(rest_kernel, rows),
        out_shape=shape(rows, ch, cols),
        in_specs=[hbm] + [vmem] * 3,
        out_specs=hbm,
        scratch_shapes=[
            pltpu.VMEM((2, 4, ch, cols), BF),
            pltpu.SemaphoreType.DMA((2,)),
        ],
        input_output_aliases={0: 0},
        compiler_params=pltpu.CompilerParams(vmem_limit_bytes=16 << 20),
        cost_estimate=pl.CostEstimate(
            flops=2 * 10**9, bytes_accessed=3 * 10**6, transcendentals=0
        ),
        name="rest",
    )(back, bwd1_spread, new_slope, slope)
    mine = pl.pallas_call(
        sum_kernel,
        out_shape=shape(devices, 8, 128),
        in_specs=[vmem],
        out_specs=vmem,
        compiler_params=pltpu.CompilerParams(vmem_limit_bytes=8 << 20),
        name="sum",
    )(parts)
    full = lax.all_to_all(mine, AXES, 0, 0, tiled=True)
    grad_w1, grad_b1, grad_w2, grad_b2 = pl.pallas_call(
        functools.partial(split_kernel, ch),
        out_shape=(
            shape(3, 3, ch, ch, dtype=F32),
            shape(1, ch, dtype=F32),
            shape(3, 3, ch, ch, dtype=F32),
            shape(1, ch, dtype=F32),
        ),
        in_specs=[vmem],
        out_specs=(vmem,) * 4,
        compiler_params=pltpu.CompilerParams(vmem_limit_bytes=8 << 20),
        name="split",
    )(full)
    return (back[None], grad_w1, grad_b1[0], grad_w2, grad_b2[0])


def solution(mesh):
    in_specs = (
        P("dp", "space", None, None),
        P("dp", "space", None, None),
        P("dp", None),
        P(),
        P(),
        P(),
        P(),
    )
    out_specs = (P("dp", "space", None, None), P(), P(), P(), P())
    return jax.shard_map(
        shards, mesh=mesh, in_specs=in_specs, out_specs=out_specs, check_vma=False
    )
```

```python
import functools
import math

import jax
import jax.numpy as jnp
from jax import lax
from jax.experimental import pallas as pl
from jax.experimental.pallas import tpu as pltpu
from jax.sharding import PartitionSpec as P

BF = jnp.bfloat16
F32 = jnp.float32
AXES = ("dp", "space")
FEAT_HALO = 3
GOAL_HALO = 1
GELU_SCALE = math.sqrt(2.0 / math.pi)
GELU_CUBE = 0.044715


def to_right(value):
    moved = pltpu.roll(value, 1, 1)
    edge = moved[:, :128]
    lane = lax.broadcasted_iota(jnp.int32, edge.shape, 1)
    edge = jnp.where(lane == 0, jnp.zeros_like(edge), edge)
    return jnp.concatenate([edge, moved[:, 128:]], axis=1)


def to_left(value):
    cols = value.shape[1]
    moved = pltpu.roll(value, cols - 1, 1)
    edge = moved[:, cols - 128 :]
    lane = lax.broadcasted_iota(jnp.int32, edge.shape, 1)
    edge = jnp.where(lane == 127, jnp.zeros_like(edge), edge)
    return jnp.concatenate([moved[:, : cols - 128], edge], axis=1)


def keep(flag, value):
    return jnp.where(flag > 0, value, jnp.zeros_like(value))


def masked(value, low, high):
    if low is None and high is None:
        return value
    half = value.shape[0] // 2
    first, second = value[:half], value[half:]
    if low is not None:
        first = keep(low, first)
    if high is not None:
        second = keep(high, second)
    return jnp.concatenate([first, second], axis=0)


def lane_sum(value):
    half = value.shape[0] // 2
    both = value[:half] + value[half:]
    total = both[:, :128]
    for start in range(128, both.shape[1], 128):
        total = total + both[:, start : start + 128]
    return total


def wave(position, channel):
    period = jnp.left_shift(jnp.full_like(channel, 4), channel & 7)
    phase = (position & (period - 1)).astype(F32)
    return jnp.sin(phase * ((2.0 * math.pi) / period.astype(F32)))


def row_waves(anchors_ref, start, half):
    shape = (half, 128)
    lane = lax.broadcasted_iota(jnp.int32, shape, 1)
    channel = lax.broadcasted_iota(jnp.int32, shape, 0)
    return wave(anchors_ref[0, 0] + start + lane, channel)


def col_waves(anchors_ref, half, cols):
    shape = (half, cols)
    lane = lax.broadcasted_iota(jnp.int32, shape, 1)
    channel = lax.broadcasted_iota(jnp.int32, shape, 0)
    return wave(anchors_ref[0, 1] + lane, channel)


def with_geo(value, row_wave, col_wave):
    rows = jnp.broadcast_to(row_wave, col_wave.shape)
    return value.astype(F32) + jnp.concatenate([rows, col_wave], axis=0)


def bias_tile(bias_ref):
    ch = bias_ref.shape[1]
    tile = jnp.transpose(jnp.broadcast_to(bias_ref[...], (128, ch)))
    return jnp.concatenate([tile, tile], axis=0)


def spread(matrix, block, mirrored=False):
    parts = jnp.dot(matrix, block, preferred_element_type=F32)
    pair = parts.shape[0] // 3
    left, right = (to_left, to_right) if mirrored else (to_right, to_left)
    return parts[pair : 2 * pair] + left(parts[:pair]) + right(parts[2 * pair :])


def activate(pre):
    square = pre * pre
    cdf = 0.5 + 0.5 * jnp.tanh(pre * (GELU_SCALE + (GELU_SCALE * GELU_CUBE) * square))
    value = pre * cdf
    bend = 2.0 * GELU_SCALE + (6.0 * GELU_SCALE * GELU_CUBE) * square
    return value, cdf + value * ((1.0 - cdf) * bend)


def view(*parts):
    def read(at, count, ch, plane=None):
        blocks = []
        for ref, start, rows in parts:
            low, high = max(at, 0), min(at + count, rows)
            if low < high:
                spot = slice((start + low) * ch, (start + high) * ch)
                blocks.append(ref[spot] if plane is None else ref[plane, spot])
            at, count = at - rows, count
        return blocks[0] if len(blocks) == 1 else jnp.concatenate(blocks, axis=0)

    return read


class Stage:
    def __init__(self, ch, cols):
        self.ch, self.cols = ch, cols

    def rows(self, at, count):
        return slice(at * self.ch, (at + count) * self.ch)

    def wide(self, tile):
        return jnp.tile(tile, (1, self.cols // 128))

    def put_three(self, target, at, value):
        spot = self.rows(at, 2)
        target[0, spot] = to_left(value)
        target[1, spot] = value
        target[2, spot] = to_right(value)

    def forward_one(self, matrix, bias, first, at, hidden, to, deriv=None, d_to=0, low=None, high=None):
        pre = spread(matrix[...], first(at, 4, self.ch)) + self.wide(bias)
        value, grad = activate(pre)
        hidden[self.rows(to, 2)] = masked(value, low, high).astype(BF)
        if deriv is not None:
            deriv[self.rows(d_to, 2)] = grad

    def forward_two(self, matrix, bias, hidden, at, goal, misfit, to, total, flag=None):
        out = spread(matrix[...], hidden(at, 4, self.ch)) + self.wide(bias)
        error = out - goal.astype(F32)
        if flag is not None:
            error = keep(flag, error)
        error = error.astype(BF)
        self.put_three(misfit, to, error)
        if flag is None:
            total[...] += lane_sum(error.astype(F32))

    def three(self, source, at, count):
        return jnp.concatenate([source(at, count, self.ch, plane) for plane in range(3)], axis=0)

    def back(self, matrix, source, at):
        return jnp.dot(matrix[...], self.three(source, at, 4), preferred_element_type=F32)

    def backward_two(self, matrix, misfit, at, deriv, d_at, slope, to, total, low=None, high=None):
        value = self.back(matrix, misfit, at) * deriv(d_at, 2, self.ch)
        value = masked(value, low, high).astype(BF)
        self.put_three(slope, to, value)
        wide = value.astype(F32)
        ch = self.ch
        if low is not None:
            wide = jnp.concatenate([jnp.zeros_like(wide[:ch]), wide[ch:]], axis=0)
        if high is not None:
            wide = jnp.concatenate([wide[:ch], jnp.zeros_like(wide[ch:])], axis=0)
        total[...] += lane_sum(wide)

    def weight_grad(self, acc, errors, e_at, source, at):
        acc[...] += lax.dot_general(
            self.three(errors, e_at, 2),
            source(at, 4, self.ch),
            (((1,), (1,)), ((), ())),
            preferred_element_type=F32,
        )


def banded(blocks):
    flat = jnp.concatenate(blocks, axis=1)
    gap = jnp.zeros(blocks[0].shape, flat.dtype)
    return jnp.concatenate(
        [jnp.concatenate([flat, gap], axis=1), jnp.concatenate([gap, flat], axis=1)], axis=0
    )


def forward_band(w_ref, j):
    return banded([w_ref[i, j].astype(F32) for i in range(3)]).astype(BF)


def backward_band(w_ref, j):
    return banded([jnp.transpose(w_ref[2 - i, j].astype(F32)) for i in range(3)]).astype(BF)


def pack_kernel(rows, feat_hbm, goal_hbm, w1_hbm, w2_hbm, even_ref, odd_ref, w1_ref, w2_ref, sems):
    odd = lax.rem(lax.axis_index("space"), 2)
    copies = []

    def start(source, target):
        copies.append(pltpu.make_async_copy(source, target, sems.at[len(copies)]))
        copies[-1].start()

    for which, ref in enumerate((even_ref, odd_ref)):
        bottom = jnp.where(odd == which, 1, 0)
        for source, count, at in ((feat_hbm, FEAT_HALO, 0), (goal_hbm, GOAL_HALO, FEAT_HALO)):
            start(source.at[pl.ds(bottom * (rows - count), count)], ref.at[at : at + count])
    start(w1_hbm, w1_ref)
    start(w2_hbm, w2_ref)
    for copy in copies:
        copy.wait()


def inner_kernel(
    rows,
    anchors_ref,
    w1_ref,
    w2_ref,
    b1_ref,
    b2_ref,
    feat,
    goal,
    back_hbm,
    first,
    hidden,
    deriv,
    misfit,
    slope,
    fwd1,
    fwd2,
    bwd2,
    bwd1_spread,
    biases,
    col_wave_ref,
    acc1,
    acc2,
    sum1,
    sum2,
    bwd1,
    back,
    sem,
):
    ch, cols = feat.shape[1:]
    half, pair = ch // 2, 2 * ch
    me = lax.axis_index("space")
    do = Stage(ch, cols)
    for j in range(3):
        spot = slice(pair * j, pair * (j + 1))
        fwd1[spot] = forward_band(w1_ref, j)
        fwd2[spot] = forward_band(w2_ref, j)
        band = backward_band(w1_ref, j)
        bwd1_spread[spot] = band
        bwd1[:, 4 * ch * j : 4 * ch * (j + 1)] = band
        bwd2[:, 4 * ch * j : 4 * ch * (j + 1)] = backward_band(w2_ref, j)
    biases[0] = bias_tile(b1_ref)
    biases[1] = bias_tile(b2_ref)
    row_wave = row_waves(anchors_ref, me * rows, half)
    col_wave_ref[...] = col_waves(anchors_ref, half, cols)
    for total in (acc1, acc2, sum1, sum2):
        total[...] = jnp.zeros_like(total)
    for row in range(rows):
        first[do.rows(row, 1)] = with_geo(
            feat[row], row_wave[:, row : row + 1], col_wave_ref[...]
        ).astype(BF)
    F, H, D = view((first, 0, rows)), view((hidden, 0, rows - 2)), view((deriv, 0, rows - 2))
    M, S = view((misfit, 0, rows - 4)), view((slope, 0, rows - 6))

    def conv_one(r):
        do.forward_one(fwd1, biases[0], F, r - 1, hidden, r - 1, deriv, r - 1)

    def conv_two(r):
        goals = jnp.concatenate([goal[r], goal[r + 1]], axis=0)
        do.forward_two(fwd2, biases[1], H, r - 2, goals, misfit, r - 2, sum2)

    def grad_two(r):
        do.weight_grad(acc2, M, r - 2, H, r - 2)

    def bend(r):
        do.backward_two(bwd2, M, r - 3, D, r - 1, slope, r - 3, sum1)

    def grad_one(r):
        do.weight_grad(acc1, S, r - 3, F, r - 1)

    def input_grad(r):
        value = do.back(bwd1, S, r - 4).astype(BF)
        back[r - 4] = value[:ch]
        back[r - 3] = value[ch:]

    steps = (
        (grad_one, 4, rows - 6, 6),
        (input_grad, 4, rows - 6, 6),
        (bend, 3, rows - 5, 4),
        (grad_two, 2, rows - 4, 3),
        (conv_two, 2, rows - 4, 2),
        (conv_one, 1, rows - 3, 0),
    )
    for turn in range(rows // 2 + 3):
        for step, low, high, lag in steps:
            r = low + 2 * (turn - lag)
            if low <= r <= high:
                step(r)
    copy = pltpu.make_async_copy(back, back_hbm.at[4 : rows - 4], sem)
    copy.start()
    copy.wait()


def edge_kernel(
    rows,
    size,
    factor,
    anchors_ref,
    fwd1,
    fwd2,
    bwd2,
    biases,
    col_wave_ref,
    old1,
    old2,
    old_sum1,
    old_sum2,
    goal,
    even_halo,
    odd_halo,
    first,
    hidden,
    deriv,
    misfit,
    slope,
    grads_ref,
    slope_out,
    even_send,
    odd_send,
    new_first,
    new_hidden,
    new_deriv,
    new_misfit,
    new_slope,
    acc1,
    acc2,
    sum1,
    sum2,
):
    ch, cols = goal.shape[1:]
    half = ch // 2
    me = lax.axis_index("space")
    above = (me > 0).astype(jnp.int32)
    below = (me < size - 1).astype(jnp.int32)
    odd = lax.rem(me, 2)
    do = Stage(ch, cols)
    flags = (above, below)

    def halo(side, k):
        return jnp.where(odd == side, odd_halo[k], even_halo[k])

    acc1[...] = old1[...]
    acc2[...] = old2[...]
    sum1[...] = old_sum1[...]
    sum2[...] = old_sum2[...]
    for side, start in enumerate((-4, rows)):
        row_wave = row_waves(anchors_ref, me * rows + start, half)
        for k in range(FEAT_HALO):
            lane = k + 1 - side
            value = with_geo(halo(side, k), row_wave[:, lane : lane + 1], col_wave_ref[...])
            new_first[side, do.rows(lane, 1)] = keep(flags[side], value).astype(BF)
        new_first[side, do.rows(FEAT_HALO * side, 1)] = jnp.zeros((ch, cols), BF)
    top, low = 0, 1
    nF, nH, nD, nM, nS = (
        [ref.at[0], ref.at[1]] for ref in (new_first, new_hidden, new_deriv, new_misfit, new_slope)
    )
    F = (view((nF[top], 0, 4), (first, 0, 5)), view((first, rows - 5, 5), (nF[low], 0, 4)))
    H = (view((nH[top], 0, 4), (hidden, 0, 2)), view((hidden, rows - 4, 2), (nH[low], 0, 4)))
    D = (view((nD[top], 0, 2), (deriv, 0, 2)), view((deriv, rows - 4, 2), (nD[low], 0, 2)))
    M = (view((nM[top], 0, 4), (misfit, 0, 2)), view((misfit, rows - 6, 2), (nM[low], 0, 4)))
    S = (view((nS[top], 0, 4), (slope, 0, 2)), view((slope, rows - 8, 2), (nS[low], 0, 4)))
    one = functools.partial(do.forward_one, fwd1, biases[0])
    one(F[top], 2, nH[top], 2, nD[top], 0, low=above)
    one(F[low], 3, nH[low], 0, nD[low], 0, high=below)
    one(F[top], 0, nH[top], 0, low=above, high=above)
    one(F[low], 5, nH[low], 2, low=below, high=below)
    two = functools.partial(do.forward_two, fwd2, biases[1])
    blank = jnp.zeros((ch, cols), BF)
    two(H[top], 2, jnp.concatenate([goal[0], goal[1]], axis=0), nM[top], 2, sum2)
    two(
        H[low], 0, jnp.concatenate([goal[rows - 2], goal[rows - 1]], axis=0), nM[low], 0, sum2
    )
    two(H[top], 0, jnp.concatenate([blank, halo(0, FEAT_HALO)], axis=0), nM[top], 0, sum2, above)
    two(H[low], 2, jnp.concatenate([halo(1, FEAT_HALO), blank], axis=0), nM[low], 2, sum2, below)
    bend = functools.partial(do.backward_two, bwd2)
    bend(M[top], 2, D[top], 2, nS[top], 2, sum1)
    bend(M[low], 0, D[low], 0, nS[low], 0, sum1)
    do.weight_grad(acc2, M[top], 2, H[top], 2)
    bend(M[top], 0, D[top], 0, nS[top], 0, sum1, low=above)
    bend(M[low], 2, D[low], 2, nS[low], 2, sum1, high=below)
    do.weight_grad(acc2, M[low], 2, H[low], 0)
    do.weight_grad(acc1, S[top], 3, F[top], 5)
    do.weight_grad(acc1, S[low], 1, F[low], 0)
    do.weight_grad(acc1, S[top], 1, F[top], 3)
    do.weight_grad(acc1, S[low], 3, F[low], 2)
    slope_out[...] = new_slope[:, 1]
    highest, lowest = new_slope[top, 1, do.rows(1, 1)], new_slope[low, 1, do.rows(2, 1)]
    even_send[...] = jnp.where(odd == 0, lowest, highest)
    odd_send[...] = jnp.where(odd == 1, lowest, highest)

    def emit(base, acc, total):
        summed = jnp.sum(total[...], axis=1, keepdims=True)
        side = jnp.broadcast_to(summed, (ch, ch))
        for j in range(3):
            upper = acc[2 * j * ch : (2 * j + 1) * ch]
            lower = acc[(2 * j + 1) * ch : (2 * j + 2) * ch]
            block = jnp.concatenate([upper[:, : 3 * ch] + lower[:, ch:], side], axis=1) * factor
            for t in range(ch // 8):
                for part in range(2):
                    grads_ref[base + (j * (ch // 8) + t) * 2 + part] = block[
                        8 * t : 8 * t + 8, 128 * part : 128 * part + 128
                    ].astype(BF)

    emit(0, acc1, sum1)
    emit(6 * (ch // 8), acc2, sum2)
    for spare in range(12 * (ch // 8), grads_ref.shape[0]):
        grads_ref[spare] = jnp.zeros((8, 128), BF)


def rest_kernel(
    rows, old_back, bwd1_spread, new_slope, slope, even_slope, odd_slope, back_hbm, back, sems
):
    ch = back.shape[2]
    odd = lax.rem(lax.axis_index("space"), 2)
    do = Stage(ch, back.shape[3])
    new, inside = [new_slope.at[0], new_slope.at[1]], slope.at[1]
    outside = [jnp.where(odd == side, odd_slope[...], even_slope[...]) for side in range(2)]
    blocks = (
        (
            jnp.concatenate([outside[0], new[0][do.rows(1, 3)]], axis=0),
            jnp.concatenate([new[0][do.rows(2, 2)], inside[do.rows(0, 2)]], axis=0),
        ),
        (
            jnp.concatenate([inside[do.rows(rows - 8, 2)], new[1][do.rows(0, 2)]], axis=0),
            jnp.concatenate([new[1][do.rows(0, 3)], outside[1]], axis=0),
        ),
    )
    copies = []
    for side, r in enumerate((0, rows - 4)):
        for at in range(2):
            value = spread(bwd1_spread[...], blocks[side][at], mirrored=True).astype(BF)
            back[side, 2 * at] = value[:ch]
            back[side, 2 * at + 1] = value[ch:]
        copy = pltpu.make_async_copy(back.at[side], back_hbm.at[r : r + 4], sems.at[side])
        copy.start()
        copies.append(copy)
    for copy in copies:
        copy.wait()


def sum_kernel(parts_ref, out_ref):
    total = jnp.sum(parts_ref[...].astype(F32), axis=0).astype(BF)
    out_ref[...] = jnp.broadcast_to(total[None], out_ref.shape)


def split_kernel(ch, full_ref, w1_ref, b1_ref, w2_ref, b2_ref):
    for base, w_ref, b_ref in ((0, w1_ref, b1_ref), (6 * (ch // 8), w2_ref, b2_ref)):
        for j in range(3):
            left, right = [
                jnp.concatenate(
                    [
                        full_ref[base + (j * (ch // 8) + t) * 2 + part].astype(F32)
                        for t in range(ch // 8)
                    ],
                    axis=0,
                )
                for part in range(2)
            ]
            w_ref[0, j] = left[:, :ch]
            w_ref[1, j] = left[:, ch:]
            w_ref[2, j] = right[:, :ch]
            if j == 0:
                b_ref[...] = jnp.transpose(right)[ch : ch + 1]


def shards(features, target, anchors, w_first, b_first, w_second, b_second):
    _, rows, ch, cols = features.shape
    size = lax.axis_size("space")
    devices = size * lax.axis_size("dp")
    factor = 1.0 / math.sqrt(features.shape[0] * devices * rows * cols)
    feats, goals = features[0], target[0]
    pair, quad = 2 * ch, 4 * ch

    links = [
        [
            link
            for low in range(first, size - 1, 2)
            for link in ((low, low + 1), (low + 1, low))
        ]
        for first in (0, 1)
    ]
    vmem = pl.BlockSpec(memory_space=pltpu.VMEM)
    smem = pl.BlockSpec(memory_space=pltpu.SMEM)
    hbm = pl.BlockSpec(memory_space=pltpu.HBM)

    def shape(*dims, dtype=BF):
        return jax.ShapeDtypeStruct(dims, dtype)

    def buffer(count, *lead, dtype=BF):
        return pltpu.VMEM(lead + (count * ch, cols), dtype)

    even_edge, odd_edge, w_first, w_second = pl.pallas_call(
        functools.partial(pack_kernel, rows),
        out_shape=(shape(FEAT_HALO + GOAL_HALO, ch, cols),) * 2 + (shape(3, 3, ch, ch),) * 2,
        in_specs=[hbm] * 4,
        out_specs=(vmem,) * 4,
        scratch_shapes=[pltpu.SemaphoreType.DMA((6,))],
        compiler_params=pltpu.CompilerParams(vmem_limit_bytes=8 << 20),
        name="pack",
    )(
        *(
            pltpu.with_memory_space_constraint(array, pltpu.HBM)
            for array in (feats, goals, w_first, w_second)
        )
    )
    odd_halo = lax.ppermute(odd_edge, "space", links[1])
    even_halo = lax.ppermute(even_edge, "space", links[0])
    (
        back,
        first,
        hidden,
        deriv,
        misfit,
        slope,
        fwd1,
        fwd2,
        bwd2,
        bwd1_spread,
        biases,
        col_wave,
        acc1,
        acc2,
        sum1,
        sum2,
    ) = pl.pallas_call(
        functools.partial(inner_kernel, rows),
        out_shape=(
            shape(rows, ch, cols),
            shape(rows * ch, cols),
            shape((rows - 2) * ch, cols),
            shape((rows - 2) * ch, cols, dtype=F32),
            shape(3, (rows - 4) * ch, cols),
            shape(3, (rows - 6) * ch, cols),
            shape(3 * pair, quad),
            shape(3 * pair, quad),
            shape(pair, 3 * quad),
            shape(3 * pair, quad),
            shape(2, pair, 128, dtype=F32),
            shape(ch // 2, cols, dtype=F32),
            shape(3 * pair, quad, dtype=F32),
            shape(3 * pair, quad, dtype=F32),
            shape(ch, 128, dtype=F32),
            shape(ch, 128, dtype=F32),
        ),
        in_specs=[smem] + [vmem] * 6,
        out_specs=(hbm,) + (vmem,) * 15,
        scratch_shapes=[
            pltpu.VMEM((pair, 3 * quad), BF),
            pltpu.VMEM((rows - 8, ch, cols), BF),
            pltpu.SemaphoreType.DMA,
        ],
        compiler_params=pltpu.CompilerParams(vmem_limit_bytes=24 << 20),
        cost_estimate=pl.CostEstimate(
            flops=14 * 10**9, bytes_accessed=12 * 10**6, transcendentals=10**6
        ),
        name="inner",
    )(
        anchors,
        w_first,
        w_second,
        b_first[None],
        b_second[None],
        feats,
        goals,
    )
    grads, new_slope, even_send, odd_send = pl.pallas_call(
        functools.partial(edge_kernel, rows, size, factor),
        out_shape=(shape(devices, 8, 128), shape(2, 4 * ch, cols)) + (shape(ch, cols),) * 2,
        in_specs=[smem] + [vmem] * 17,
        out_specs=(vmem,) * 4,
        scratch_shapes=[
            buffer(4, 2),
            buffer(4, 2),
            buffer(2, 2, dtype=F32),
            buffer(4, 2, 3),
            buffer(4, 2, 3),
            pltpu.VMEM((3 * pair, quad), F32),
            pltpu.VMEM((3 * pair, quad), F32),
            pltpu.VMEM((ch, 128), F32),
            pltpu.VMEM((ch, 128), F32),
        ],
        compiler_params=pltpu.CompilerParams(vmem_limit_bytes=24 << 20),
        cost_estimate=pl.CostEstimate(
            flops=9 * 10**9, bytes_accessed=10 * 10**6, transcendentals=5 * 10**5
        ),
        name="edges",
    )(
        anchors,
        fwd1,
        fwd2,
        bwd2,
        biases,
        col_wave,
        acc1,
        acc2,
        sum1,
        sum2,
        goals,
        even_halo,
        odd_halo,
        first,
        hidden,
        deriv,
        misfit,
        slope,
    )
    parts = lax.all_to_all(grads, AXES, 0, 0, tiled=True)
    odd_slope = lax.ppermute(odd_send, "space", links[1])
    even_slope = lax.ppermute(even_send, "space", links[0])
    back = pl.pallas_call(
        functools.partial(rest_kernel, rows),
        out_shape=shape(rows, ch, cols),
        in_specs=[hbm] + [vmem] * 5,
        out_specs=hbm,
        scratch_shapes=[
            pltpu.VMEM((2, 4, ch, cols), BF),
            pltpu.SemaphoreType.DMA((2,)),
        ],
        input_output_aliases={0: 0},
        compiler_params=pltpu.CompilerParams(vmem_limit_bytes=16 << 20),
        cost_estimate=pl.CostEstimate(
            flops=2 * 10**9, bytes_accessed=3 * 10**6, transcendentals=0
        ),
        name="rest",
    )(back, bwd1_spread, new_slope, slope, even_slope, odd_slope)
    mine = pl.pallas_call(
        sum_kernel,
        out_shape=shape(devices, 8, 128),
        in_specs=[vmem],
        out_specs=vmem,
        compiler_params=pltpu.CompilerParams(vmem_limit_bytes=8 << 20),
        name="sum",
    )(parts)
    full = lax.all_to_all(mine, AXES, 0, 0, tiled=True)
    grad_w1, grad_b1, grad_w2, grad_b2 = pl.pallas_call(
        functools.partial(split_kernel, ch),
        out_shape=(
            shape(3, 3, ch, ch, dtype=F32),
            shape(1, ch, dtype=F32),
            shape(3, 3, ch, ch, dtype=F32),
            shape(1, ch, dtype=F32),
        ),
        in_specs=[vmem],
        out_specs=(vmem,) * 4,
        compiler_params=pltpu.CompilerParams(vmem_limit_bytes=8 << 20),
        name="split",
    )(full)
    return (back[None], grad_w1, grad_b1[0], grad_w2, grad_b2[0])


def solution(mesh):
    in_specs = (
        P("dp", "space", None, None),
        P("dp", "space", None, None),
        P("dp", None),
        P(),
        P(),
        P(),
        P(),
    )
    out_specs = (P("dp", "space", None, None), P(), P(), P(), P())
    return jax.shard_map(
        shards, mesh=mesh, in_specs=in_specs, out_specs=out_specs, check_vma=False
    )
```

```python
import functools
import math

import jax
import jax.numpy as jnp
from jax import lax
from jax.experimental import pallas as pl
from jax.experimental.pallas import tpu as pltpu
from jax.sharding import PartitionSpec as P

BF = jnp.bfloat16
F32 = jnp.float32
AXES = ("dp", "space")
FEAT_HALO = 3
GOAL_HALO = 1
GELU_SCALE = math.sqrt(2.0 / math.pi)
GELU_CUBE = 0.044715


def to_right(value):
    moved = pltpu.roll(value, 1, 1)
    edge = moved[:, :128]
    lane = lax.broadcasted_iota(jnp.int32, edge.shape, 1)
    edge = jnp.where(lane == 0, jnp.zeros_like(edge), edge)
    return jnp.concatenate([edge, moved[:, 128:]], axis=1)


def to_left(value):
    cols = value.shape[1]
    moved = pltpu.roll(value, cols - 1, 1)
    edge = moved[:, cols - 128 :]
    lane = lax.broadcasted_iota(jnp.int32, edge.shape, 1)
    edge = jnp.where(lane == 127, jnp.zeros_like(edge), edge)
    return jnp.concatenate([moved[:, : cols - 128], edge], axis=1)


def keep(flag, value):
    return jnp.where(flag > 0, value, jnp.zeros_like(value))


def masked(value, low, high):
    if low is None and high is None:
        return value
    half = value.shape[0] // 2
    first, second = value[:half], value[half:]
    if low is not None:
        first = keep(low, first)
    if high is not None:
        second = keep(high, second)
    return jnp.concatenate([first, second], axis=0)


def lane_sum(value):
    half = value.shape[0] // 2
    both = value[:half] + value[half:]
    total = both[:, :128]
    for start in range(128, both.shape[1], 128):
        total = total + both[:, start : start + 128]
    return total


def wave(position, channel):
    period = jnp.left_shift(jnp.full_like(channel, 4), channel & 7)
    phase = (position & (period - 1)).astype(F32)
    return jnp.sin(phase * ((2.0 * math.pi) / period.astype(F32)))


def row_waves(anchors_ref, start, half):
    shape = (half, 128)
    lane = lax.broadcasted_iota(jnp.int32, shape, 1)
    channel = lax.broadcasted_iota(jnp.int32, shape, 0)
    return wave(anchors_ref[0, 0] + start + lane, channel)


def col_waves(anchors_ref, half, cols):
    shape = (half, cols)
    lane = lax.broadcasted_iota(jnp.int32, shape, 1)
    channel = lax.broadcasted_iota(jnp.int32, shape, 0)
    return wave(anchors_ref[0, 1] + lane, channel)


def with_geo(value, row_wave, col_wave):
    rows = jnp.broadcast_to(row_wave, col_wave.shape)
    return value.astype(F32) + jnp.concatenate([rows, col_wave], axis=0)


def bias_tile(bias_ref):
    ch = bias_ref.shape[1]
    tile = jnp.transpose(jnp.broadcast_to(bias_ref[...], (128, ch)))
    return jnp.concatenate([tile, tile], axis=0)


def spread(matrix, block, mirrored=False):
    parts = jnp.dot(matrix, block, preferred_element_type=F32)
    pair = parts.shape[0] // 3
    left, right = (to_left, to_right) if mirrored else (to_right, to_left)
    return parts[pair : 2 * pair] + left(parts[:pair]) + right(parts[2 * pair :])


def activate(pre):
    square = pre * pre
    cdf = 0.5 + 0.5 * jnp.tanh(pre * (GELU_SCALE + (GELU_SCALE * GELU_CUBE) * square))
    value = pre * cdf
    bend = 2.0 * GELU_SCALE + (6.0 * GELU_SCALE * GELU_CUBE) * square
    return value, cdf + value * ((1.0 - cdf) * bend)


def view(*parts):
    def read(at, count, ch, plane=None):
        blocks = []
        for ref, start, rows in parts:
            low, high = max(at, 0), min(at + count, rows)
            if low < high:
                spot = slice((start + low) * ch, (start + high) * ch)
                blocks.append(ref[spot] if plane is None else ref[plane, spot])
            at, count = at - rows, count
        return blocks[0] if len(blocks) == 1 else jnp.concatenate(blocks, axis=0)

    return read


class Stage:
    def __init__(self, ch, cols):
        self.ch, self.cols = ch, cols

    def rows(self, at, count):
        return slice(at * self.ch, (at + count) * self.ch)

    def wide(self, tile):
        return jnp.tile(tile, (1, self.cols // 128))

    def put_three(self, target, at, value):
        spot = self.rows(at, value.shape[0] // self.ch)
        target[0, spot] = to_left(value)
        target[1, spot] = value
        target[2, spot] = to_right(value)

    def forward_one(self, matrix, bias, first, at, hidden, to, deriv=None, d_to=0, low=None, high=None):
        pre = spread(matrix[...], first(at, 4, self.ch)) + self.wide(bias)
        value, grad = activate(pre)
        hidden[self.rows(to, 2)] = masked(value, low, high).astype(BF)
        if deriv is not None:
            deriv[self.rows(d_to, 2)] = grad

    def forward_two(self, matrix, bias, hidden, at, goal, misfit, to, total, flag=None):
        out = spread(matrix[...], hidden(at, 4, self.ch)) + self.wide(bias)
        error = out - goal.astype(F32)
        if flag is not None:
            error = keep(flag, error)
        error = error.astype(BF)
        self.put_three(misfit, to, error)
        if flag is None:
            total[...] += lane_sum(error.astype(F32))

    def one_row(self, matrix, bias, source, at, which):
        ch = self.ch
        bands = [matrix[(2 * j + which) * ch : (2 * j + which + 1) * ch] for j in range(3)]
        return spread(jnp.concatenate(bands, axis=0), source(at, 4, ch)) + self.wide(bias[:ch])

    def three(self, source, at, count):
        return jnp.concatenate([source(at, count, self.ch, plane) for plane in range(3)], axis=0)

    def back(self, matrix, source, at):
        return jnp.dot(matrix[...], self.three(source, at, 4), preferred_element_type=F32)

    def backward_two(self, matrix, misfit, at, deriv, d_at, slope, to, total, low=None, high=None):
        value = self.back(matrix, misfit, at) * deriv(d_at, 2, self.ch)
        value = masked(value, low, high).astype(BF)
        self.put_three(slope, to, value)
        wide = value.astype(F32)
        ch = self.ch
        if low is not None:
            wide = jnp.concatenate([jnp.zeros_like(wide[:ch]), wide[ch:]], axis=0)
        if high is not None:
            wide = jnp.concatenate([wide[:ch], jnp.zeros_like(wide[ch:])], axis=0)
        total[...] += lane_sum(wide)

    def weight_grad(self, acc, errors, e_at, source, at):
        acc[...] += lax.dot_general(
            self.three(errors, e_at, 2),
            source(at, 4, self.ch),
            (((1,), (1,)), ((), ())),
            preferred_element_type=F32,
        )


def banded(blocks):
    flat = jnp.concatenate(blocks, axis=1)
    gap = jnp.zeros(blocks[0].shape, flat.dtype)
    return jnp.concatenate(
        [jnp.concatenate([flat, gap], axis=1), jnp.concatenate([gap, flat], axis=1)], axis=0
    )


def forward_band(w_ref, j):
    return banded([w_ref[i, j].astype(F32) for i in range(3)]).astype(BF)


def backward_band(w_ref, j):
    return banded([jnp.transpose(w_ref[2 - i, j].astype(F32)) for i in range(3)]).astype(BF)


def pack_kernel(rows, feat_hbm, goal_hbm, w1_hbm, w2_hbm, even_ref, odd_ref, w1_ref, w2_ref, sems):
    odd = lax.rem(lax.axis_index("space"), 2)
    copies = []

    def start(source, target):
        copies.append(pltpu.make_async_copy(source, target, sems.at[len(copies)]))
        copies[-1].start()

    for which, ref in enumerate((even_ref, odd_ref)):
        bottom = jnp.where(odd == which, 1, 0)
        for source, count, at in ((feat_hbm, FEAT_HALO, 0), (goal_hbm, GOAL_HALO, FEAT_HALO)):
            start(source.at[pl.ds(bottom * (rows - count), count)], ref.at[at : at + count])
    start(w1_hbm, w1_ref)
    start(w2_hbm, w2_ref)
    for copy in copies:
        copy.wait()


def inner_kernel(
    rows,
    anchors_ref,
    w1_ref,
    w2_ref,
    b1_ref,
    b2_ref,
    feat,
    goal,
    back_hbm,
    first,
    hidden,
    deriv,
    misfit,
    slope,
    fwd1,
    fwd2,
    bwd2,
    bwd1_spread,
    biases,
    col_wave_ref,
    acc1,
    acc2,
    sum1,
    sum2,
    bwd1,
    back,
    sem,
):
    ch, cols = feat.shape[1:]
    half, pair = ch // 2, 2 * ch
    me = lax.axis_index("space")
    do = Stage(ch, cols)
    for j in range(3):
        spot = slice(pair * j, pair * (j + 1))
        fwd1[spot] = forward_band(w1_ref, j)
        fwd2[spot] = forward_band(w2_ref, j)
        band = backward_band(w1_ref, j)
        bwd1_spread[spot] = band
        bwd1[:, 4 * ch * j : 4 * ch * (j + 1)] = band
        bwd2[:, 4 * ch * j : 4 * ch * (j + 1)] = backward_band(w2_ref, j)
    biases[0] = bias_tile(b1_ref)
    biases[1] = bias_tile(b2_ref)
    row_wave = row_waves(anchors_ref, me * rows, half)
    col_wave_ref[...] = col_waves(anchors_ref, half, cols)
    for total in (acc1, acc2, sum1, sum2):
        total[...] = jnp.zeros_like(total)
    for row in range(rows):
        first[do.rows(row, 1)] = with_geo(
            feat[row], row_wave[:, row : row + 1], col_wave_ref[...]
        ).astype(BF)
    F, H, D = view((first, 0, rows)), view((hidden, 0, rows - 2)), view((deriv, 0, rows - 2))
    M, S = view((misfit, 0, rows - 4)), view((slope, 0, rows - 6))

    def conv_one(r):
        do.forward_one(fwd1, biases[0], F, r - 1, hidden, r - 1, deriv, r - 1)

    def conv_two(r):
        goals = jnp.concatenate([goal[r], goal[r + 1]], axis=0)
        do.forward_two(fwd2, biases[1], H, r - 2, goals, misfit, r - 2, sum2)

    def grad_two(r):
        do.weight_grad(acc2, M, r - 2, H, r - 2)

    def bend(r):
        do.backward_two(bwd2, M, r - 3, D, r - 1, slope, r - 3, sum1)

    def grad_one(r):
        do.weight_grad(acc1, S, r - 3, F, r - 1)

    def input_grad(r):
        value = do.back(bwd1, S, r - 4).astype(BF)
        back[r - 4] = value[:ch]
        back[r - 3] = value[ch:]

    steps = (
        (grad_one, 4, rows - 6, 6),
        (input_grad, 4, rows - 6, 6),
        (bend, 3, rows - 5, 4),
        (grad_two, 2, rows - 4, 3),
        (conv_two, 2, rows - 4, 2),
        (conv_one, 1, rows - 3, 0),
    )
    for turn in range(rows // 2 + 3):
        for step, low, high, lag in steps:
            r = low + 2 * (turn - lag)
            if low <= r <= high:
                step(r)
    copy = pltpu.make_async_copy(back, back_hbm.at[4 : rows - 4], sem)
    copy.start()
    copy.wait()


def edge_kernel(
    rows,
    size,
    factor,
    anchors_ref,
    fwd1,
    fwd2,
    bwd2,
    biases,
    col_wave_ref,
    old1,
    old2,
    old_sum1,
    old_sum2,
    goal,
    even_halo,
    odd_halo,
    first,
    hidden,
    deriv,
    misfit,
    slope,
    grads_ref,
    slope_out,
    even_send,
    odd_send,
    new_first,
    new_hidden,
    new_deriv,
    new_misfit,
    new_slope,
    acc1,
    acc2,
    sum1,
    sum2,
):
    ch, cols = goal.shape[1:]
    half = ch // 2
    me = lax.axis_index("space")
    above = (me > 0).astype(jnp.int32)
    below = (me < size - 1).astype(jnp.int32)
    odd = lax.rem(me, 2)
    do = Stage(ch, cols)
    flags = (above, below)

    def halo(side, k):
        return jnp.where(odd == side, odd_halo[k], even_halo[k])

    acc1[...] = old1[...]
    acc2[...] = old2[...]
    sum1[...] = old_sum1[...]
    sum2[...] = old_sum2[...]
    for side, start in enumerate((-4, rows)):
        row_wave = row_waves(anchors_ref, me * rows + start, half)
        for k in range(FEAT_HALO):
            lane = k + 1 - side
            value = with_geo(halo(side, k), row_wave[:, lane : lane + 1], col_wave_ref[...])
            new_first[side, do.rows(lane, 1)] = keep(flags[side], value).astype(BF)
        new_first[side, do.rows(FEAT_HALO * side, 1)] = jnp.zeros((ch, cols), BF)
    top, low = 0, 1
    nF, nH, nD, nM, nS = (
        [ref.at[0], ref.at[1]] for ref in (new_first, new_hidden, new_deriv, new_misfit, new_slope)
    )
    F = (view((nF[top], 0, 4), (first, 0, 5)), view((first, rows - 5, 5), (nF[low], 0, 4)))
    H = (view((nH[top], 0, 4), (hidden, 0, 2)), view((hidden, rows - 4, 2), (nH[low], 0, 4)))
    D = (view((nD[top], 0, 2), (deriv, 0, 2)), view((deriv, rows - 4, 2), (nD[low], 0, 2)))
    M = (view((nM[top], 0, 4), (misfit, 0, 2)), view((misfit, rows - 6, 2), (nM[low], 0, 4)))
    S = (view((nS[top], 0, 4), (slope, 0, 2)), view((slope, rows - 8, 2), (nS[low], 0, 4)))
    one = functools.partial(do.forward_one, fwd1, biases[0])
    one(F[top], 2, nH[top], 2, nD[top], 0, low=above)
    one(F[low], 3, nH[low], 0, nD[low], 0, high=below)
    blank = jnp.zeros((ch, cols), BF)
    ends = ((top, 0, 1, 1, 0), (low, 5, 0, 2, 3))
    for side, at, which, to, spare in ends:
        value = activate(do.one_row(fwd1, biases[0], F[side], at, which))[0]
        nH[side][do.rows(to, 1)] = keep(flags[side], value).astype(BF)
        nH[side][do.rows(spare, 1)] = blank
    two = functools.partial(do.forward_two, fwd2, biases[1])
    two(H[top], 2, jnp.concatenate([goal[0], goal[1]], axis=0), nM[top], 2, sum2)
    two(
        H[low], 0, jnp.concatenate([goal[rows - 2], goal[rows - 1]], axis=0), nM[low], 0, sum2
    )
    for side, at, which, to, spare in ((top, 0, 1, 1, 0), (low, 2, 0, 2, 3)):
        out = do.one_row(fwd2, biases[1], H[side], at, which)
        error = keep(flags[side], out - halo(side, FEAT_HALO).astype(F32))
        do.put_three(nM[side], to, error.astype(BF))
        do.put_three(nM[side], spare, blank)
    bend = functools.partial(do.backward_two, bwd2)
    bend(M[top], 2, D[top], 2, nS[top], 2, sum1)
    bend(M[low], 0, D[low], 0, nS[low], 0, sum1)
    do.weight_grad(acc2, M[top], 2, H[top], 2)
    bend(M[top], 0, D[top], 0, nS[top], 0, sum1, low=above)
    bend(M[low], 2, D[low], 2, nS[low], 2, sum1, high=below)
    do.weight_grad(acc2, M[low], 2, H[low], 0)
    do.weight_grad(acc1, S[top], 3, F[top], 5)
    do.weight_grad(acc1, S[low], 1, F[low], 0)
    do.weight_grad(acc1, S[top], 1, F[top], 3)
    do.weight_grad(acc1, S[low], 3, F[low], 2)
    slope_out[...] = new_slope[:, 1]
    highest, lowest = new_slope[top, 1, do.rows(1, 1)], new_slope[low, 1, do.rows(2, 1)]
    even_send[...] = jnp.where(odd == 0, lowest, highest)
    odd_send[...] = jnp.where(odd == 1, lowest, highest)

    def emit(base, acc, total):
        summed = jnp.sum(total[...], axis=1, keepdims=True)
        side = jnp.broadcast_to(summed, (ch, ch))
        for j in range(3):
            upper = acc[2 * j * ch : (2 * j + 1) * ch]
            lower = acc[(2 * j + 1) * ch : (2 * j + 2) * ch]
            block = jnp.concatenate([upper[:, : 3 * ch] + lower[:, ch:], side], axis=1) * factor
            for t in range(ch // 8):
                for part in range(2):
                    grads_ref[base + (j * (ch // 8) + t) * 2 + part] = block[
                        8 * t : 8 * t + 8, 128 * part : 128 * part + 128
                    ].astype(BF)

    emit(0, acc1, sum1)
    emit(6 * (ch // 8), acc2, sum2)
    for spare in range(12 * (ch // 8), grads_ref.shape[0]):
        grads_ref[spare] = jnp.zeros((8, 128), BF)


def rest_kernel(
    rows, old_back, bwd1_spread, new_slope, slope, even_slope, odd_slope, back_hbm, back, sems
):
    ch = back.shape[2]
    odd = lax.rem(lax.axis_index("space"), 2)
    do = Stage(ch, back.shape[3])
    new, inside = [new_slope.at[0], new_slope.at[1]], slope.at[1]
    outside = [jnp.where(odd == side, odd_slope[...], even_slope[...]) for side in range(2)]
    blocks = (
        (
            jnp.concatenate([outside[0], new[0][do.rows(1, 3)]], axis=0),
            jnp.concatenate([new[0][do.rows(2, 2)], inside[do.rows(0, 2)]], axis=0),
        ),
        (
            jnp.concatenate([inside[do.rows(rows - 8, 2)], new[1][do.rows(0, 2)]], axis=0),
            jnp.concatenate([new[1][do.rows(0, 3)], outside[1]], axis=0),
        ),
    )
    copies = []
    for side, r in enumerate((0, rows - 4)):
        for at in range(2):
            value = spread(bwd1_spread[...], blocks[side][at], mirrored=True).astype(BF)
            back[side, 2 * at] = value[:ch]
            back[side, 2 * at + 1] = value[ch:]
        copy = pltpu.make_async_copy(back.at[side], back_hbm.at[r : r + 4], sems.at[side])
        copy.start()
        copies.append(copy)
    for copy in copies:
        copy.wait()


def sum_kernel(parts_ref, out_ref):
    total = jnp.sum(parts_ref[...].astype(F32), axis=0).astype(BF)
    out_ref[...] = jnp.broadcast_to(total[None], out_ref.shape)


def split_kernel(ch, full_ref, w1_ref, b1_ref, w2_ref, b2_ref):
    for base, w_ref, b_ref in ((0, w1_ref, b1_ref), (6 * (ch // 8), w2_ref, b2_ref)):
        for j in range(3):
            left, right = [
                jnp.concatenate(
                    [
                        full_ref[base + (j * (ch // 8) + t) * 2 + part].astype(F32)
                        for t in range(ch // 8)
                    ],
                    axis=0,
                )
                for part in range(2)
            ]
            w_ref[0, j] = left[:, :ch]
            w_ref[1, j] = left[:, ch:]
            w_ref[2, j] = right[:, :ch]
            if j == 0:
                b_ref[...] = jnp.transpose(right)[ch : ch + 1]


def shards(features, target, anchors, w_first, b_first, w_second, b_second):
    _, rows, ch, cols = features.shape
    size = lax.axis_size("space")
    devices = size * lax.axis_size("dp")
    factor = 1.0 / math.sqrt(features.shape[0] * devices * rows * cols)
    feats, goals = features[0], target[0]
    pair, quad = 2 * ch, 4 * ch

    links = [
        [
            link
            for low in range(first, size - 1, 2)
            for link in ((low, low + 1), (low + 1, low))
        ]
        for first in (0, 1)
    ]
    vmem = pl.BlockSpec(memory_space=pltpu.VMEM)
    smem = pl.BlockSpec(memory_space=pltpu.SMEM)
    hbm = pl.BlockSpec(memory_space=pltpu.HBM)

    def shape(*dims, dtype=BF):
        return jax.ShapeDtypeStruct(dims, dtype)

    def buffer(count, *lead, dtype=BF):
        return pltpu.VMEM(lead + (count * ch, cols), dtype)

    even_edge, odd_edge, w_first, w_second = pl.pallas_call(
        functools.partial(pack_kernel, rows),
        out_shape=(shape(FEAT_HALO + GOAL_HALO, ch, cols),) * 2 + (shape(3, 3, ch, ch),) * 2,
        in_specs=[hbm] * 4,
        out_specs=(vmem,) * 4,
        scratch_shapes=[pltpu.SemaphoreType.DMA((6,))],
        compiler_params=pltpu.CompilerParams(vmem_limit_bytes=8 << 20),
        name="pack",
    )(
        *(
            pltpu.with_memory_space_constraint(array, pltpu.HBM)
            for array in (feats, goals, w_first, w_second)
        )
    )
    odd_halo = lax.ppermute(odd_edge, "space", links[1])
    even_halo = lax.ppermute(even_edge, "space", links[0])
    (
        back,
        first,
        hidden,
        deriv,
        misfit,
        slope,
        fwd1,
        fwd2,
        bwd2,
        bwd1_spread,
        biases,
        col_wave,
        acc1,
        acc2,
        sum1,
        sum2,
    ) = pl.pallas_call(
        functools.partial(inner_kernel, rows),
        out_shape=(
            shape(rows, ch, cols),
            shape(rows * ch, cols),
            shape((rows - 2) * ch, cols),
            shape((rows - 2) * ch, cols, dtype=F32),
            shape(3, (rows - 4) * ch, cols),
            shape(3, (rows - 6) * ch, cols),
            shape(3 * pair, quad),
            shape(3 * pair, quad),
            shape(pair, 3 * quad),
            shape(3 * pair, quad),
            shape(2, pair, 128, dtype=F32),
            shape(ch // 2, cols, dtype=F32),
            shape(3 * pair, quad, dtype=F32),
            shape(3 * pair, quad, dtype=F32),
            shape(ch, 128, dtype=F32),
            shape(ch, 128, dtype=F32),
        ),
        in_specs=[smem] + [vmem] * 6,
        out_specs=(hbm,) + (vmem,) * 15,
        scratch_shapes=[
            pltpu.VMEM((pair, 3 * quad), BF),
            pltpu.VMEM((rows - 8, ch, cols), BF),
            pltpu.SemaphoreType.DMA,
        ],
        compiler_params=pltpu.CompilerParams(vmem_limit_bytes=24 << 20),
        cost_estimate=pl.CostEstimate(
            flops=14 * 10**9, bytes_accessed=12 * 10**6, transcendentals=10**6
        ),
        name="inner",
    )(
        anchors,
        w_first,
        w_second,
        b_first[None],
        b_second[None],
        feats,
        goals,
    )
    grads, new_slope, even_send, odd_send = pl.pallas_call(
        functools.partial(edge_kernel, rows, size, factor),
        out_shape=(shape(devices, 8, 128), shape(2, 4 * ch, cols)) + (shape(ch, cols),) * 2,
        in_specs=[smem] + [vmem] * 17,
        out_specs=(vmem,) * 4,
        scratch_shapes=[
            buffer(4, 2),
            buffer(4, 2),
            buffer(2, 2, dtype=F32),
            buffer(4, 2, 3),
            buffer(4, 2, 3),
            pltpu.VMEM((3 * pair, quad), F32),
            pltpu.VMEM((3 * pair, quad), F32),
            pltpu.VMEM((ch, 128), F32),
            pltpu.VMEM((ch, 128), F32),
        ],
        compiler_params=pltpu.CompilerParams(vmem_limit_bytes=24 << 20),
        cost_estimate=pl.CostEstimate(
            flops=9 * 10**9, bytes_accessed=10 * 10**6, transcendentals=5 * 10**5
        ),
        name="edges",
    )(
        anchors,
        fwd1,
        fwd2,
        bwd2,
        biases,
        col_wave,
        acc1,
        acc2,
        sum1,
        sum2,
        goals,
        even_halo,
        odd_halo,
        first,
        hidden,
        deriv,
        misfit,
        slope,
    )
    parts = lax.all_to_all(grads, AXES, 0, 0, tiled=True)
    odd_slope = lax.ppermute(odd_send, "space", links[1])
    even_slope = lax.ppermute(even_send, "space", links[0])
    back = pl.pallas_call(
        functools.partial(rest_kernel, rows),
        out_shape=shape(rows, ch, cols),
        in_specs=[hbm] + [vmem] * 5,
        out_specs=hbm,
        scratch_shapes=[
            pltpu.VMEM((2, 4, ch, cols), BF),
            pltpu.SemaphoreType.DMA((2,)),
        ],
        input_output_aliases={0: 0},
        compiler_params=pltpu.CompilerParams(vmem_limit_bytes=16 << 20),
        cost_estimate=pl.CostEstimate(
            flops=2 * 10**9, bytes_accessed=3 * 10**6, transcendentals=0
        ),
        name="rest",
    )(back, bwd1_spread, new_slope, slope, even_slope, odd_slope)
    mine = pl.pallas_call(
        sum_kernel,
        out_shape=shape(devices, 8, 128),
        in_specs=[vmem],
        out_specs=vmem,
        compiler_params=pltpu.CompilerParams(vmem_limit_bytes=8 << 20),
        name="sum",
    )(parts)
    full = lax.all_to_all(mine, AXES, 0, 0, tiled=True)
    grad_w1, grad_b1, grad_w2, grad_b2 = pl.pallas_call(
        functools.partial(split_kernel, ch),
        out_shape=(
            shape(3, 3, ch, ch, dtype=F32),
            shape(1, ch, dtype=F32),
            shape(3, 3, ch, ch, dtype=F32),
            shape(1, ch, dtype=F32),
        ),
        in_specs=[vmem],
        out_specs=(vmem,) * 4,
        compiler_params=pltpu.CompilerParams(vmem_limit_bytes=8 << 20),
        name="split",
    )(full)
    return (back[None], grad_w1, grad_b1[0], grad_w2, grad_b2[0])


def solution(mesh):
    in_specs = (
        P("dp", "space", None, None),
        P("dp", "space", None, None),
        P("dp", None),
        P(),
        P(),
        P(),
        P(),
    )
    out_specs = (P("dp", "space", None, None), P(), P(), P(), P())
    return jax.shard_map(
        shards, mesh=mesh, in_specs=in_specs, out_specs=out_specs, check_vma=False
    )
```
